256 devices in a mesh: down: 64 (over x_lo, y, z), cross: 4 (over x_hi, core).
Axes of the slice: x: 4 (x_hi: 2, x_lo: 2; x = x_hi * 2 + x_lo), y: 4, z: 8, core: 2. Of those that a mesh axis runs over, the one named last changes fastest.
Arguments:
- positions: float32 [3, 128, 32, 128], P(None, 'down', 'cross'), may hold values from 0 to 1
- velocities: float32 [3, 128, 32, 128], P(None, 'down', 'cross'), may hold values from -3 to 3
- plastic_viscosity: float32 [128, 32, 128], P('down', 'cross'), may hold values from 0.3 to 3
- yield_stress: float32 [128, 32, 128], P('down', 'cross'), may hold values from 0.3 to 3
- counts: int32 [128, 32], P('down', 'cross'), may hold values from 1 to 128, as said below
- moving: int32 [128, 32], P('down', 'cross'), may hold values from 0 to 32, as said below
Outputs:
- new_positions: float32 [3, 128, 32, 128], P(None, 'down', 'cross')
- new_velocities: float32 [3, 128, 32, 128], P(None, 'down', 'cross')
The draws below stay inside these ranges and needn't reach their ends.
Inputs may be any that keep to these rules, and one draw needn't show every extreme that they name: At least one; the first counts slots of a block are its live particles; 128 is reached in every draw. Never more than counts of the same block; counts minus moving of a block plus moving of the block just upslope is at most 128; both 32 and that bound of 128 are reached in every draw.
All inputs are finite; a program needn't handle non-finite values.
Results may differ from the reference program's by a relative error of at most 0.0001.
Values sent between devices are 32-bit elements; how exact they have to be, the bound alone decides.
A program may use at most 64 MiB of HBM per device.

```python
import math
import jax
import jax.numpy as jnp
from jax import lax

SLOTS = 128
MOVE_MAX = 32
JACOBI = 2
BLOCKS_DOWN = 128
BLOCKS_CROSS = 32


def occupancy_plan(key):
    base_key = jax.random.fold_in(key, 1701)
    key_list = jax.random.split(base_key, 5)
    moving_count = jax.random.randint(key_list[0], (BLOCKS_DOWN, BLOCKS_CROSS), 0, MOVE_MAX + 1)
    level_row = jax.random.randint(key_list[1], (BLOCKS_DOWN, 1), 48, SLOTS - MOVE_MAX + 1)
    spread = jax.random.randint(key_list[2], (BLOCKS_DOWN, BLOCKS_CROSS), 0, SLOTS - MOVE_MAX)
    keep_count = 1 + spread * (level_row - 1) // (SLOTS - MOVE_MAX)
    row_pick = jax.random.randint(key_list[3], (), 0, BLOCKS_DOWN - 1)
    col_pick = jax.random.randint(key_list[4], (), 0, BLOCKS_CROSS)
    row_ids = lax.broadcasted_iota(jnp.int32, (BLOCKS_DOWN, BLOCKS_CROSS), 0)
    col_ids = lax.broadcasted_iota(jnp.int32, (BLOCKS_DOWN, BLOCKS_CROSS), 1)
    at_pick = (row_ids == row_pick) & (col_ids == col_pick)
    below_pick = (row_ids == row_pick + 1) & (col_ids == col_pick)
    moving_count = jnp.where(at_pick, MOVE_MAX, moving_count)
    keep_count = jnp.where(at_pick | below_pick, SLOTS - MOVE_MAX, keep_count)
    return ((keep_count + moving_count).astype(jnp.int32), moving_count.astype(jnp.int32))


def draw_counts(key, part):
    return occupancy_plan(key)[0]


def draw_moving(key, part):
    return occupancy_plan(key)[1]


def shard_levels(stream_key, extent, shards, smallest, largest):
    gain = 1.0
    for position, parts in shards:
        draws = jax.random.uniform(jax.random.fold_in(jax.random.fold_in(stream_key, 6), position), (parts,), jnp.float32, smallest / len(shards), largest / len(shards))
        gain = gain * jnp.repeat(jnp.exp(draws), extent[position] // parts).reshape((-1,) + (1,) * (len(extent) - 1 - position))
    return gain


def normal_values(own_key, extent, width, limit, pieces=(), kind=jnp.bfloat16):
    level = shard_levels(own_key, extent, pieces, -0.22, 0.18) if pieces else 1.0
    values = jax.random.normal(own_key, extent, jnp.float32) * width * level
    return jnp.minimum(jnp.maximum(values, -limit), limit).astype(kind)


def setup_inputs(seed: int = 0) -> dict:
    arg_keys = jax.random.split(jax.random.key(seed), 7)
    positions = jnp.clip(1.0 * jax.random.uniform(arg_keys[0], (3, BLOCKS_DOWN, BLOCKS_CROSS, SLOTS), jnp.float32) ** shard_levels(arg_keys[0], (3, BLOCKS_DOWN, BLOCKS_CROSS, SLOTS), ((1, 64), (2, 4)), -0.2, 0.2), 0.0, 1.0)
    velocities = normal_values(arg_keys[1], (3, BLOCKS_DOWN, BLOCKS_CROSS, SLOTS), 0.5, 3.0, ((1, 64), (2, 4)), jnp.float32)
    plastic_viscosity = jnp.clip(jnp.exp(math.log(3.0) - 2.3025851 * jax.random.uniform(arg_keys[2], (BLOCKS_DOWN, BLOCKS_CROSS, SLOTS), jnp.float32) ** shard_levels(arg_keys[2], (BLOCKS_DOWN, BLOCKS_CROSS, SLOTS), ((0, 64), (1, 4)), -0.2, 0.2)), 0.3, 3.0)
    yield_stress = jnp.clip(jnp.exp(math.log(3.0) - 2.3025851 * jax.random.uniform(arg_keys[3], (BLOCKS_DOWN, BLOCKS_CROSS, SLOTS), jnp.float32) ** shard_levels(arg_keys[3], (BLOCKS_DOWN, BLOCKS_CROSS, SLOTS), ((0, 64), (1, 4)), -0.2, 0.2)), 0.3, 3.0)
    counts = draw_counts(jax.random.fold_in(arg_keys[6], 71), 0)
    moving = draw_moving(jax.random.fold_in(arg_keys[6], 71), 0)
    return {"positions": positions, "velocities": velocities, "plastic_viscosity": plastic_viscosity, "yield_stress": yield_stress, "counts": counts, "moving": moving}


KERNEL_NORM = 21.0 / (2.0 * math.pi)
PARTICLE_MASS = 0.02
REST_DENSITY = 1.0
STIFFNESS = 2.0
TIME_STEP = 0.05
GRAVITY_DOWN = 0.5
GRAVITY_UP = -1.0
NEIGHBOUR_STEPS = [(-1, -1), (-1, 0), (-1, 1), (0, -1), (0, 0), (0, 1), (1, -1), (1, 0), (1, 1)]

def take_row(padded, lead_blocks, row_index, step_down, step_cross, col_count):
    whole_row = lax.dynamic_index_in_dim(padded, row_index + lead_blocks + step_down, axis=1, keepdims=False)
    return whole_row[:, lead_blocks + step_cross:lead_blocks + step_cross + col_count, :]

def separation(target, source, step_down, step_cross):
    offsets = (float(step_down), float(step_cross), 0.0)
    separations = [source[component][:, None, :] - target[component][:, :, None] + offsets[component] for component in range(3)]
    distance = jnp.sqrt(separations[0] * separations[0] + separations[1] * separations[1] + separations[2] * separations[2])
    falloff = jnp.maximum(1.0 - distance, 0.0)
    falloff_cubed = falloff * falloff * falloff
    weight = KERNEL_NORM * falloff_cubed * falloff * (4.0 * distance + 1.0)
    strength = 20.0 * KERNEL_NORM * falloff_cubed
    return (separations, weight, strength)

def density_pass(state_pad, lead_blocks, row_count, col_count):
    slot_count = state_pad.shape[3]

    def one_row(row_index):
        target = take_row(state_pad, lead_blocks, row_index, 0, 0, col_count)
        kernel_sum = jnp.zeros((col_count, slot_count), jnp.float32)
        strain = jnp.zeros((col_count, slot_count), jnp.float32)
        for step_down, step_cross in NEIGHBOUR_STEPS:
            source = take_row(state_pad, lead_blocks, row_index, step_down, step_cross, col_count)
            separations, weight, strength = separation(target, source, step_down, step_cross)
            present = source[6][:, None, :]
            spread = jnp.zeros_like(weight)
            for component in range(3):
                change = source[3 + component][:, None, :] - target[3 + component][:, :, None]
                spread = spread + change * change
            kernel_sum = kernel_sum + lax.optimization_barrier(jnp.sum(present * weight, axis=2))
            strain = strain + lax.optimization_barrier(jnp.sum(present * strength * spread, axis=2))
        density = PARTICLE_MASS * (kernel_sum + KERNEL_NORM * (1.0 - target[6]))
        return jnp.stack([density, PARTICLE_MASS * strain])
    result = lax.map(one_row, jnp.arange(row_count, dtype=jnp.int32))
    return jnp.moveaxis(result, 0, 1)

def force_pass(state_pad, state_lead, dens_pad, dens_lead, row_count, col_count):
    slot_count = state_pad.shape[3]

    def one_row(row_index):
        target = take_row(state_pad, state_lead, row_index, 0, 0, col_count)
        target_dens = take_row(dens_pad, dens_lead, row_index, 0, 0, col_count)
        totals = [jnp.zeros((col_count, slot_count), jnp.float32) for component in range(4)]
        for step_down, step_cross in NEIGHBOUR_STEPS:
            source = take_row(state_pad, state_lead, row_index, step_down, step_cross, col_count)
            source_dens = take_row(dens_pad, dens_lead, row_index, step_down, step_cross, col_count)
            separations, weight, strength = separation(target, source, step_down, step_cross)
            present = source[6][:, None, :]
            pressure_push = present * (target_dens[1][:, :, None] + source_dens[1][:, None, :]) * strength
            for component in range(3):
                totals[component] = totals[component] - lax.optimization_barrier(jnp.sum(pressure_push * separations[component], axis=2))
            coupling = present * (target_dens[2][:, :, None] + source_dens[2][:, None, :]) * strength * target_dens[0][:, :, None] * source_dens[0][:, None, :]
            totals[3] = totals[3] + lax.optimization_barrier(jnp.sum(coupling, axis=2))
        return PARTICLE_MASS * jnp.stack(totals)
    result = lax.map(one_row, jnp.arange(row_count, dtype=jnp.int32))
    return jnp.moveaxis(result, 0, 1)

def jacobi_pass(state_pad, state_lead, dens_pad, dens_lead, speed_pad, row_count, col_count):
    slot_count = state_pad.shape[3]

    def one_row(row_index):
        target = take_row(state_pad, state_lead, row_index, 0, 0, col_count)
        target_dens = take_row(dens_pad, dens_lead, row_index, 0, 0, col_count)
        totals = [jnp.zeros((col_count, slot_count), jnp.float32) for component in range(3)]
        for step_down, step_cross in NEIGHBOUR_STEPS:
            source = take_row(state_pad, state_lead, row_index, step_down, step_cross, col_count)
            source_dens = take_row(dens_pad, dens_lead, row_index, step_down, step_cross, col_count)
            source_speed = take_row(speed_pad, 1, row_index, step_down, step_cross, col_count)
            separations, weight, strength = separation(target, source, step_down, step_cross)
            present = source[6][:, None, :]
            coupling = present * (target_dens[2][:, :, None] + source_dens[2][:, None, :]) * strength * target_dens[0][:, :, None] * source_dens[0][:, None, :]
            for component in range(3):
                totals[component] = totals[component] + lax.optimization_barrier(jnp.sum(coupling * source_speed[component][:, None, :], axis=2))
        return PARTICLE_MASS * jnp.stack(totals)
    result = lax.map(one_row, jnp.arange(row_count, dtype=jnp.int32))
    return jnp.moveaxis(result, 0, 1)

def pack_departing(field_six, keep_count, moving_count):
    move_slots = MOVE_MAX
    offsets = lax.broadcasted_iota(jnp.int32, keep_count.shape + (move_slots,), 2)
    index = jnp.minimum(keep_count[..., None] + offsets, field_six.shape[3] - 1)
    taken = jnp.take_along_axis(field_six, jnp.broadcast_to(index[None], (6,) + index.shape), axis=3)
    shifted = jnp.concatenate([taken[:1] - 1.0, taken[1:]], axis=0)
    valid = (offsets < moving_count[..., None]).astype(jnp.float32)
    return shifted * valid[None]

def place_arrivals(field_six, keep_count, arrivals, arriving):
    slot_ids = lax.broadcasted_iota(jnp.int32, field_six.shape[1:], 2)
    relative = slot_ids - keep_count[..., None]
    index = jnp.clip(relative, 0, arrivals.shape[3] - 1)
    incoming = jnp.take_along_axis(arrivals, jnp.broadcast_to(index[None], (6,) + index.shape), axis=3)
    own_mask = (slot_ids < keep_count[..., None]).astype(jnp.float32)
    new_mask = ((relative >= 0) & (relative < arriving[..., None])).astype(jnp.float32)
    return field_six * own_mask[None] + incoming * new_mask[None]

def pad_cycle(field):
    return jnp.pad(field, ((0, 0), (1, 1), (1, 1), (0, 0)))

def reference(positions, velocities, plastic_viscosity, yield_stress, counts, moving):
    row_count, col_count, slot_count = positions.shape[1:]
    slot_ids = lax.broadcasted_iota(jnp.int32, (row_count, col_count, slot_count), 2)
    live = (slot_ids < counts[:, :, None]).astype(jnp.float32)
    state = jnp.concatenate([positions, velocities, live[None]], axis=0)
    state_pad = pad_cycle(state)
    density_strain = density_pass(state_pad, 1, row_count, col_count)
    inverse = 1.0 / density_strain[0]
    pressure = STIFFNESS * (density_strain[0] - REST_DENSITY) * inverse * inverse
    viscosity = plastic_viscosity + yield_stress / jnp.sqrt(1.0 + density_strain[1])
    dens_pad = pad_cycle(jnp.stack([inverse, pressure, viscosity]))
    forces = force_pass(state_pad, 1, dens_pad, 1, row_count, col_count)
    gravity = jnp.array([GRAVITY_DOWN, 0.0, GRAVITY_UP], jnp.float32)[:, None, None, None]
    predicted = velocities + TIME_STEP * (forces[:3] + gravity)
    diagonal = 1.0 + TIME_STEP * forces[3]
    current = predicted
    for sweep_index in range(JACOBI):
        pulled = jacobi_pass(state_pad, 1, dens_pad, 1, pad_cycle(current), row_count, col_count)
        current = (predicted + TIME_STEP * pulled) / diagonal
    moved_positions = positions + TIME_STEP * current
    field_six = jnp.concatenate([moved_positions, current], axis=0)
    keep_count = counts - moving
    packed = pack_departing(field_six, keep_count, moving)
    arrivals = jnp.concatenate([jnp.zeros_like(packed[:, :1]), packed[:, :-1]], axis=1)
    arriving = jnp.concatenate([jnp.zeros_like(moving[:1]), moving[:-1]], axis=0)
    result = place_arrivals(field_six, keep_count, arrivals, arriving)
    return (result[:3], result[3:])
```

```python
import math

import jax
import jax.numpy as jnp
from jax import lax
from jax.sharding import PartitionSpec as P

MOVE_MAX = 32
JACOBI = 2


KERNEL_NORM = 21.0 / (2.0 * math.pi)
PARTICLE_MASS = 0.02
REST_DENSITY = 1.0
STIFFNESS = 2.0
TIME_STEP = 0.05
GRAVITY_DOWN = 0.5
GRAVITY_UP = -1.0
NEIGHBOUR_STEPS = [(-1, -1), (-1, 0), (-1, 1), (0, -1), (0, 0), (0, 1), (1, -1), (1, 0), (1, 1)]


def with_halo(array, sides, width):
    for axis, dim in sides:
        count, length = (lax.axis_size(axis), array.shape[dim])
        up = [(i, (i + 1) % count) for i in range(count - 1)]
        down = [(j, i) for i, j in up]
        last = lax.slice_in_dim(array, length - width, length, axis=dim)
        initial = lax.slice_in_dim(array, 0, width, axis=dim)
        before = lax.ppermute(last, axis, up)
        after = lax.ppermute(initial, axis, down)
        array = jnp.concatenate([before, array, after], axis=dim)
    return array


def from_behind(block, axis, distance):
    devices = range(lax.axis_size(axis))
    route = [(i - distance, i) for i in devices if i - distance in devices]
    return lax.ppermute(block, axis, route)


def take_row(padded, lead_blocks, row_index, step_down, step_cross, col_count):
    whole_row = lax.dynamic_index_in_dim(
        padded, row_index + lead_blocks + step_down, axis=1, keepdims=False
    )
    return whole_row[:, lead_blocks + step_cross : lead_blocks + step_cross + col_count, :]


def separation(target, source, step_down, step_cross):
    offsets = (float(step_down), float(step_cross), 0.0)
    separations = [
        source[component][:, None, :] - target[component][:, :, None] + offsets[component]
        for component in range(3)
    ]
    distance = jnp.sqrt(
        separations[0] * separations[0]
        + separations[1] * separations[1]
        + separations[2] * separations[2]
    )
    falloff = jnp.maximum(1.0 - distance, 0.0)
    falloff_cubed = falloff * falloff * falloff
    weight = KERNEL_NORM * falloff_cubed * falloff * (4.0 * distance + 1.0)
    strength = 20.0 * KERNEL_NORM * falloff_cubed
    return (separations, weight, strength)


def density_pass(state_pad, lead_blocks, row_count, col_count):
    slot_count = state_pad.shape[3]

    def density_one_row(row_index):
        target = take_row(state_pad, lead_blocks, row_index, 0, 0, col_count)
        kernel_sum = jnp.zeros((col_count, slot_count), jnp.float32)
        strain = jnp.zeros((col_count, slot_count), jnp.float32)
        for step_down, step_cross in NEIGHBOUR_STEPS:
            source = take_row(state_pad, lead_blocks, row_index, step_down, step_cross, col_count)
            separations, weight, strength = separation(target, source, step_down, step_cross)
            present = source[6][:, None, :]
            spread = jnp.zeros_like(weight)
            for component in range(3):
                change = source[3 + component][:, None, :] - target[3 + component][:, :, None]
                spread = spread + change * change
            kernel_sum = kernel_sum + jnp.sum(present * weight, axis=2)
            strain = strain + jnp.sum(present * strength * spread, axis=2)
        density = PARTICLE_MASS * (kernel_sum + KERNEL_NORM * (1.0 - target[6]))
        return jnp.stack([density, PARTICLE_MASS * strain])

    result = lax.map(density_one_row, jnp.arange(row_count, dtype=jnp.int32))
    return jnp.moveaxis(result, 0, 1)


def force_pass(state_pad, state_lead, dens_pad, dens_lead, row_count, col_count):
    slot_count = state_pad.shape[3]

    def force_one_row(row_index):
        target = take_row(state_pad, state_lead, row_index, 0, 0, col_count)
        target_dens = take_row(dens_pad, dens_lead, row_index, 0, 0, col_count)
        totals = [jnp.zeros((col_count, slot_count), jnp.float32) for component in range(4)]
        for step_down, step_cross in NEIGHBOUR_STEPS:
            source = take_row(state_pad, state_lead, row_index, step_down, step_cross, col_count)
            source_dens = take_row(dens_pad, dens_lead, row_index, step_down, step_cross, col_count)
            separations, weight, strength = separation(target, source, step_down, step_cross)
            present = source[6][:, None, :]
            pressure_push = (
                present * (target_dens[1][:, :, None] + source_dens[1][:, None, :]) * strength
            )
            for component in range(3):
                totals[component] = totals[component] - jnp.sum(
                    pressure_push * separations[component], axis=2
                )
            coupling = (
                present
                * (target_dens[2][:, :, None] + source_dens[2][:, None, :])
                * strength
                * target_dens[0][:, :, None]
                * source_dens[0][:, None, :]
            )
            totals[3] = totals[3] + jnp.sum(coupling, axis=2)
        return PARTICLE_MASS * jnp.stack(totals)

    result = lax.map(force_one_row, jnp.arange(row_count, dtype=jnp.int32))
    return jnp.moveaxis(result, 0, 1)


def jacobi_pass(state_pad, state_lead, dens_pad, dens_lead, speed_pad, row_count, col_count):
    slot_count = state_pad.shape[3]

    def jacobi_one_row(row_index):
        target = take_row(state_pad, state_lead, row_index, 0, 0, col_count)
        target_dens = take_row(dens_pad, dens_lead, row_index, 0, 0, col_count)
        totals = [jnp.zeros((col_count, slot_count), jnp.float32) for component in range(3)]
        for step_down, step_cross in NEIGHBOUR_STEPS:
            source = take_row(state_pad, state_lead, row_index, step_down, step_cross, col_count)
            source_dens = take_row(dens_pad, dens_lead, row_index, step_down, step_cross, col_count)
            source_speed = take_row(speed_pad, 1, row_index, step_down, step_cross, col_count)
            separations, weight, strength = separation(target, source, step_down, step_cross)
            present = source[6][:, None, :]
            coupling = (
                present
                * (target_dens[2][:, :, None] + source_dens[2][:, None, :])
                * strength
                * target_dens[0][:, :, None]
                * source_dens[0][:, None, :]
            )
            for component in range(3):
                totals[component] = totals[component] + jnp.sum(
                    coupling * source_speed[component][:, None, :], axis=2
                )
        return PARTICLE_MASS * jnp.stack(totals)

    result = lax.map(jacobi_one_row, jnp.arange(row_count, dtype=jnp.int32))
    return jnp.moveaxis(result, 0, 1)


def shift_lanes(field, distance):
    slot_count = field.shape[-1]
    step = 1
    while step < slot_count:
        rolled = jnp.roll(field, -step, axis=-1)
        chosen = ((distance & step) != 0)[None, :, :, None]
        field = jnp.where(chosen, rolled, field)
        step *= 2
    return field


def place_arrivals(field_six, keep_count, moving):
    slot_count = field_six.shape[3]
    keep_plane = jnp.broadcast_to(keep_count[-1].astype(jnp.float32)[:, None], field_six.shape[2:])
    move_plane = jnp.broadcast_to(moving[-1].astype(jnp.float32)[:, None], field_six.shape[2:])
    edge_pack = jnp.concatenate([field_six[:, -1], keep_plane[None], move_plane[None]], axis=0)
    received = from_behind(edge_pack, "down", 1)
    source_field = jnp.concatenate([received[:6][:, None], field_six[:, :-1]], axis=1)
    source_keep = jnp.concatenate([received[6, :, 0].astype(jnp.int32)[None], keep_count[:-1]], axis=0)
    arriving = jnp.concatenate([received[7, :, 0].astype(jnp.int32)[None], moving[:-1]], axis=0)
    distance = jnp.mod(source_keep - keep_count, slot_count)
    incoming = shift_lanes(source_field, distance)
    incoming = jnp.concatenate([incoming[:1] - 1.0, incoming[1:]], axis=0)
    slot_ids = lax.broadcasted_iota(jnp.int32, field_six.shape[1:], 2)
    own_mask = slot_ids < keep_count[..., None]
    new_mask = (slot_ids >= keep_count[..., None]) & (
        slot_ids < (keep_count + arriving)[..., None]
    )
    return jnp.where(own_mask[None], field_six, jnp.where(new_mask[None], incoming, 0.0))


def per_device(positions, velocities, plastic_viscosity, yield_stress, counts, moving):
    row_count, col_count, slot_count = positions.shape[1:]
    slot_ids = lax.broadcasted_iota(jnp.int32, (row_count, col_count, slot_count), 2)
    live = (slot_ids < counts[:, :, None]).astype(jnp.float32)
    state = jnp.concatenate([positions, velocities, live[None]], axis=0)
    state_pad = with_halo(state, (("down", 1), ("cross", 2)), 1)
    state_lead = 1
    density_strain = density_pass(state_pad, 1, row_count, col_count)
    inverse = 1.0 / density_strain[0]
    pressure = STIFFNESS * (density_strain[0] - REST_DENSITY) * inverse * inverse
    viscosity = plastic_viscosity + yield_stress / jnp.sqrt(1.0 + density_strain[1])
    dens_pad = with_halo(jnp.stack([inverse, pressure, viscosity]), (("down", 1), ("cross", 2)), 1)
    forces = force_pass(state_pad, state_lead, dens_pad, 1, row_count, col_count)
    gravity = jnp.array([GRAVITY_DOWN, 0.0, GRAVITY_UP], jnp.float32)[:, None, None, None]
    predicted = velocities + TIME_STEP * (forces[:3] + gravity)
    diagonal = 1.0 + TIME_STEP * forces[3]
    current = predicted
    for sweep_index in range(JACOBI):
        speed_pad = with_halo(current, (("down", 1), ("cross", 2)), 1)
        pulled = jacobi_pass(state_pad, state_lead, dens_pad, 1, speed_pad, row_count, col_count)
        current = (predicted + TIME_STEP * pulled) / diagonal
    moved_positions = positions + TIME_STEP * current
    field_six = jnp.concatenate([moved_positions, current], axis=0)
    keep_count = counts - moving
    result = place_arrivals(field_six, keep_count, moving)
    return (result[:3], result[3:])


def solution(mesh):
    return jax.shard_map(
        per_device,
        mesh=mesh,
        in_specs=(
            P(None, "down", "cross", None),
            P(None, "down", "cross", None),
            P("down", "cross", None),
            P("down", "cross", None),
            P("down", "cross"),
            P("down", "cross"),
        ),
        out_specs=(P(None, "down", "cross", None), P(None, "down", "cross", None)),
        check_vma=False,
    )
```

```python
import math

import jax
import jax.numpy as jnp
from jax import lax
from jax.experimental import pallas as pl
from jax.sharding import PartitionSpec as P

MOVE_MAX = 32
JACOBI = 2


KERNEL_NORM = 21.0 / (2.0 * math.pi)
PARTICLE_MASS = 0.02
REST_DENSITY = 1.0
STIFFNESS = 2.0
TIME_STEP = 0.05
GRAVITY_DOWN = 0.5
GRAVITY_UP = -1.0
NEIGHBOUR_STEPS = [(-1, -1), (-1, 0), (-1, 1), (0, -1), (0, 0), (0, 1), (1, -1), (1, 0), (1, 1)]


def with_halo(array, sides, width):
    for axis, dim in sides:
        count, length = (lax.axis_size(axis), array.shape[dim])
        up = [(i, (i + 1) % count) for i in range(count - 1)]
        down = [(j, i) for i, j in up]
        last = lax.slice_in_dim(array, length - width, length, axis=dim)
        initial = lax.slice_in_dim(array, 0, width, axis=dim)
        before = lax.ppermute(last, axis, up)
        after = lax.ppermute(initial, axis, down)
        array = jnp.concatenate([before, array, after], axis=dim)
    return array


def from_behind(block, axis, distance):
    devices = range(lax.axis_size(axis))
    route = [(i - distance, i) for i in devices if i - distance in devices]
    return lax.ppermute(block, axis, route)


def take_row(padded, lead_blocks, row_index, step_down, step_cross, col_count):
    whole_row = lax.dynamic_index_in_dim(
        padded, row_index + lead_blocks + step_down, axis=1, keepdims=False
    )
    return whole_row[:, lead_blocks + step_cross : lead_blocks + step_cross + col_count, :]


def separation(target, source, step_down, step_cross):
    offsets = (float(step_down), float(step_cross), 0.0)
    separations = [
        source[component][:, None, :] - target[component][:, :, None] + offsets[component]
        for component in range(3)
    ]
    distance = jnp.sqrt(
        separations[0] * separations[0]
        + separations[1] * separations[1]
        + separations[2] * separations[2]
    )
    falloff = jnp.maximum(1.0 - distance, 0.0)
    falloff_cubed = falloff * falloff * falloff
    weight = KERNEL_NORM * falloff_cubed * falloff * (4.0 * distance + 1.0)
    strength = 20.0 * KERNEL_NORM * falloff_cubed
    return (separations, weight, strength)


FAR_AWAY = 1.0e4
CHUNK = 16


def pair_pass(kind, target, source, row_count, col_count):
    slot_count = target.shape[-1]
    block_count = row_count * col_count
    chunk_count = slot_count // CHUNK
    padded_cols = col_count + 2
    target_count = target.shape[0]
    source_count = source.shape[0]
    output_count = {"density": 2, "force": 4, "jacobi": 3}[kind]
    target_cols = jnp.moveaxis(target.reshape(target_count, block_count, slot_count), 0, 2)
    source_rows = source.reshape(source_count, (row_count + 2) * padded_cols, slot_count)

    def kernel(target_ref, source_ref, out_ref):
        def body(step, carry):
            block = step // chunk_count
            first = pl.multiple_of((step % chunk_count) * CHUNK, CHUNK)
            row = block // col_count
            col = block % col_count
            own = target_ref[block, pl.ds(first, CHUNK), :]
            mine = [
                jnp.broadcast_to(own[:, k : k + 1], (CHUNK, slot_count)) for k in range(target_count)
            ]
            totals = [jnp.zeros((CHUNK, slot_count), jnp.float32) for k in range(output_count)]
            for step_down, step_cross in NEIGHBOUR_STEPS:
                near = (row + 1 + step_down) * padded_cols + (col + 1 + step_cross)
                other = [source_ref[k, pl.ds(near, 1), :] for k in range(source_count)]
                gaps = [
                    other[0] + float(step_down) - mine[0],
                    other[1] + float(step_cross) - mine[1],
                    other[2] - mine[2],
                ]
                distance = jnp.sqrt(gaps[0] * gaps[0] + gaps[1] * gaps[1] + gaps[2] * gaps[2])
                falloff = jnp.maximum(1.0 - distance, 0.0)
                cubed = falloff * falloff * falloff
                if kind == "density":
                    totals[0] = totals[0] + cubed * falloff * (4.0 * distance + 1.0)
                    spread = None
                    for k in range(3):
                        change = other[3 + k] - mine[3 + k]
                        term = change * change
                        spread = term if spread is None else spread + term
                    totals[1] = totals[1] + cubed * spread
                elif kind == "force":
                    push = (mine[3] + other[3]) * cubed
                    for k in range(3):
                        totals[k] = totals[k] + push * gaps[k]
                    totals[3] = totals[3] + (mine[4] + other[5]) * other[4] * cubed
                else:
                    pull = (mine[3] + other[3]) * cubed
                    for k in range(3):
                        totals[k] = totals[k] + pull * other[4 + k]
            for k in range(output_count):
                out_ref[block, pl.ds(first, CHUNK), pl.ds(k, 1)] = jnp.sum(
                    totals[k], axis=1, keepdims=True
                )
            return carry

        lax.fori_loop(0, block_count * chunk_count, body, 0)

    result = pl.pallas_call(
        kernel,
        out_shape=jax.ShapeDtypeStruct((block_count, slot_count, output_count), jnp.float32),
    )(target_cols, source_rows)
    return jnp.moveaxis(result, 2, 0).reshape(output_count, row_count, col_count, slot_count)


def shift_lanes(field, distance):
    slot_count = field.shape[-1]
    step = 1
    while step < slot_count:
        rolled = jnp.roll(field, -step, axis=-1)
        chosen = ((distance & step) != 0)[None, :, :, None]
        field = jnp.where(chosen, rolled, field)
        step *= 2
    return field


def place_arrivals(field_six, keep_count, moving):
    slot_count = field_six.shape[3]
    keep_plane = jnp.broadcast_to(keep_count[-1].astype(jnp.float32)[:, None], field_six.shape[2:])
    move_plane = jnp.broadcast_to(moving[-1].astype(jnp.float32)[:, None], field_six.shape[2:])
    edge_pack = jnp.concatenate([field_six[:, -1], keep_plane[None], move_plane[None]], axis=0)
    received = from_behind(edge_pack, "down", 1)
    source_field = jnp.concatenate([received[:6][:, None], field_six[:, :-1]], axis=1)
    source_keep = jnp.concatenate([received[6, :, 0].astype(jnp.int32)[None], keep_count[:-1]], axis=0)
    arriving = jnp.concatenate([received[7, :, 0].astype(jnp.int32)[None], moving[:-1]], axis=0)
    distance = jnp.mod(source_keep - keep_count, slot_count)
    incoming = shift_lanes(source_field, distance)
    incoming = jnp.concatenate([incoming[:1] - 1.0, incoming[1:]], axis=0)
    slot_ids = lax.broadcasted_iota(jnp.int32, field_six.shape[1:], 2)
    own_mask = slot_ids < keep_count[..., None]
    new_mask = (slot_ids >= keep_count[..., None]) & (
        slot_ids < (keep_count + arriving)[..., None]
    )
    return jnp.where(own_mask[None], field_six, jnp.where(new_mask[None], incoming, 0.0))


def per_device(positions, velocities, plastic_viscosity, yield_stress, counts, moving):
    row_count, col_count, slot_count = positions.shape[1:]
    slot_ids = lax.broadcasted_iota(jnp.int32, (row_count, col_count, slot_count), 2)
    live = (slot_ids < counts[:, :, None]).astype(jnp.float32)
    state = jnp.concatenate([positions, velocities, live[None]], axis=0)
    state_pad = with_halo(state, (("down", 1), ("cross", 2)), 1)
    far = jnp.where(state_pad[6:7] > 0.0, state_pad[:3], FAR_AWAY)
    sums = pair_pass(
        "density",
        jnp.concatenate([positions, velocities], axis=0),
        jnp.concatenate([far, state_pad[3:6]], axis=0),
        row_count,
        col_count,
    )
    density = PARTICLE_MASS * (KERNEL_NORM * sums[0] + KERNEL_NORM * (1.0 - live))
    strain = (PARTICLE_MASS * 20.0 * KERNEL_NORM) * sums[1]
    inverse = 1.0 / density
    pressure = STIFFNESS * (density - REST_DENSITY) * inverse * inverse
    viscosity = plastic_viscosity + yield_stress / jnp.sqrt(1.0 + strain)
    dens_pad = with_halo(jnp.stack([inverse, pressure, viscosity]), (("down", 1), ("cross", 2)), 1)
    forces = pair_pass(
        "force",
        jnp.concatenate([positions, pressure[None], viscosity[None]], axis=0),
        jnp.concatenate([far, dens_pad[1:2], dens_pad[0:1], dens_pad[2:3]], axis=0),
        row_count,
        col_count,
    )
    scale = PARTICLE_MASS * 20.0 * KERNEL_NORM
    gravity = jnp.array([GRAVITY_DOWN, 0.0, GRAVITY_UP], jnp.float32)[:, None, None, None]
    predicted = velocities + TIME_STEP * (-scale * forces[:3] + gravity)
    diagonal = 1.0 + TIME_STEP * (scale * inverse * forces[3])
    target = jnp.concatenate([positions, viscosity[None]], axis=0)
    current = predicted
    for sweep_index in range(JACOBI):
        speed_pad = with_halo(current, (("down", 1), ("cross", 2)), 1)
        pulled = pair_pass(
            "jacobi",
            target,
            jnp.concatenate([far, dens_pad[2:3], speed_pad * dens_pad[0:1]], axis=0),
            row_count,
            col_count,
        )
        current = (predicted + TIME_STEP * (scale * inverse * pulled)) / diagonal
    moved_positions = positions + TIME_STEP * current
    field_six = jnp.concatenate([moved_positions, current], axis=0)
    keep_count = counts - moving
    result = place_arrivals(field_six, keep_count, moving)
    return (result[:3], result[3:])


def solution(mesh):
    return jax.shard_map(
        per_device,
        mesh=mesh,
        in_specs=(
            P(None, "down", "cross", None),
            P(None, "down", "cross", None),
            P("down", "cross", None),
            P("down", "cross", None),
            P("down", "cross"),
            P("down", "cross"),
        ),
        out_specs=(P(None, "down", "cross", None), P(None, "down", "cross", None)),
        check_vma=False,
    )
```

```python
import math

import jax
import jax.numpy as jnp
from jax import lax
from jax.experimental import pallas as pl
from jax.sharding import PartitionSpec as P

MOVE_MAX = 32
JACOBI = 2


KERNEL_NORM = 21.0 / (2.0 * math.pi)
PARTICLE_MASS = 0.02
REST_DENSITY = 1.0
STIFFNESS = 2.0
TIME_STEP = 0.05
GRAVITY_DOWN = 0.5
GRAVITY_UP = -1.0
NEIGHBOUR_STEPS = [(-1, -1), (-1, 0), (-1, 1), (0, -1), (0, 0), (0, 1), (1, -1), (1, 0), (1, 1)]


def with_halo(array):
    down_count, cross_count = (lax.axis_size("down"), lax.axis_size("cross"))
    row_count, col_count = array.shape[1:3]
    spans = {-1: (row_count - 1, col_count - 1), 0: (0, 0), 1: (0, 0)}
    sizes = {-1: (1, 1), 0: (row_count, col_count), 1: (1, 1)}

    def fetch(step_down, step_cross):
        piece = lax.slice_in_dim(
            array, spans[step_down][0], spans[step_down][0] + sizes[step_down][0], axis=1
        )
        piece = lax.slice_in_dim(
            piece, spans[step_cross][1], spans[step_cross][1] + sizes[step_cross][1], axis=2
        )
        route = []
        for down_index in range(down_count):
            for cross_index in range(cross_count):
                source_down, source_cross = (down_index + step_down, cross_index + step_cross)
                if 0 <= source_down < down_count and 0 <= source_cross < cross_count:
                    route.append(
                        (source_down * cross_count + source_cross, down_index * cross_count + cross_index)
                    )
        return lax.ppermute(piece, ("down", "cross"), route)

    grid = [
        [array if (step_down, step_cross) == (0, 0) else fetch(step_down, step_cross) for step_cross in (-1, 0, 1)]
        for step_down in (-1, 0, 1)
    ]
    return jnp.concatenate([jnp.concatenate(row, axis=2) for row in grid], axis=1)


def from_behind(block, axis, distance):
    devices = range(lax.axis_size(axis))
    route = [(i - distance, i) for i in devices if i - distance in devices]
    return lax.ppermute(block, axis, route)


def take_row(padded, lead_blocks, row_index, step_down, step_cross, col_count):
    whole_row = lax.dynamic_index_in_dim(
        padded, row_index + lead_blocks + step_down, axis=1, keepdims=False
    )
    return whole_row[:, lead_blocks + step_cross : lead_blocks + step_cross + col_count, :]


def separation(target, source, step_down, step_cross):
    offsets = (float(step_down), float(step_cross), 0.0)
    separations = [
        source[component][:, None, :] - target[component][:, :, None] + offsets[component]
        for component in range(3)
    ]
    distance = jnp.sqrt(
        separations[0] * separations[0]
        + separations[1] * separations[1]
        + separations[2] * separations[2]
    )
    falloff = jnp.maximum(1.0 - distance, 0.0)
    falloff_cubed = falloff * falloff * falloff
    weight = KERNEL_NORM * falloff_cubed * falloff * (4.0 * distance + 1.0)
    strength = 20.0 * KERNEL_NORM * falloff_cubed
    return (separations, weight, strength)


FAR_AWAY = 1.0e4
CHUNK = 16


def pair_pass(kind, target, source, row_count, col_count):
    slot_count = target.shape[-1]
    block_count = row_count * col_count
    chunk_count = slot_count // CHUNK
    padded_cols = col_count + 2
    target_count = target.shape[0]
    source_count = source.shape[0]
    output_count = {"density": 2, "force": 4, "jacobi": 3}[kind]
    target_cols = jnp.moveaxis(target.reshape(target_count, block_count, slot_count), 0, 2)
    source_rows = source.reshape(source_count, (row_count + 2) * padded_cols, slot_count)

    def kernel(target_ref, source_ref, out_ref):
        def body(step, carry):
            block = step // chunk_count
            first = pl.multiple_of((step % chunk_count) * CHUNK, CHUNK)
            row = block // col_count
            col = block % col_count
            own = target_ref[block, pl.ds(first, CHUNK), :]
            mine = [
                jnp.broadcast_to(own[:, k : k + 1], (CHUNK, slot_count)) for k in range(target_count)
            ]
            totals = [jnp.zeros((CHUNK, slot_count), jnp.float32) for k in range(output_count)]
            for step_down, step_cross in NEIGHBOUR_STEPS:
                near = (row + 1 + step_down) * padded_cols + (col + 1 + step_cross)
                other = [source_ref[k, pl.ds(near, 1), :] for k in range(source_count)]
                gaps = [
                    other[0] + float(step_down) - mine[0],
                    other[1] + float(step_cross) - mine[1],
                    other[2] - mine[2],
                ]
                distance = jnp.sqrt(gaps[0] * gaps[0] + gaps[1] * gaps[1] + gaps[2] * gaps[2])
                falloff = jnp.maximum(1.0 - distance, 0.0)
                cubed = falloff * falloff * falloff
                if kind == "density":
                    totals[0] = totals[0] + cubed * falloff * (4.0 * distance + 1.0)
                    spread = None
                    for k in range(3):
                        change = other[3 + k] - mine[3 + k]
                        term = change * change
                        spread = term if spread is None else spread + term
                    totals[1] = totals[1] + cubed * spread
                elif kind == "force":
                    push = (mine[3] + other[3]) * cubed
                    for k in range(3):
                        totals[k] = totals[k] + push * gaps[k]
                    totals[3] = totals[3] + (mine[4] + other[5]) * other[4] * cubed
                else:
                    pull = (mine[3] + other[3]) * cubed
                    for k in range(3):
                        totals[k] = totals[k] + pull * other[4 + k]
            for k in range(output_count):
                out_ref[block, pl.ds(first, CHUNK), pl.ds(k, 1)] = jnp.sum(
                    totals[k], axis=1, keepdims=True
                )
            return carry

        lax.fori_loop(0, block_count * chunk_count, body, 0)

    result = pl.pallas_call(
        kernel,
        out_shape=jax.ShapeDtypeStruct((block_count, slot_count, output_count), jnp.float32),
    )(target_cols, source_rows)
    return jnp.moveaxis(result, 2, 0).reshape(output_count, row_count, col_count, slot_count)


def shift_lanes(field, distance):
    slot_count = field.shape[-1]
    step = 1
    while step < slot_count:
        rolled = jnp.roll(field, -step, axis=-1)
        chosen = ((distance & step) != 0)[None, :, :, None]
        field = jnp.where(chosen, rolled, field)
        step *= 2
    return field


def place_arrivals(field_six, keep_count, moving):
    slot_count = field_six.shape[3]
    keep_plane = jnp.broadcast_to(keep_count[-1].astype(jnp.float32)[:, None], field_six.shape[2:])
    move_plane = jnp.broadcast_to(moving[-1].astype(jnp.float32)[:, None], field_six.shape[2:])
    edge_pack = jnp.concatenate([field_six[:, -1], keep_plane[None], move_plane[None]], axis=0)
    received = from_behind(edge_pack, "down", 1)
    source_field = jnp.concatenate([received[:6][:, None], field_six[:, :-1]], axis=1)
    source_keep = jnp.concatenate([received[6, :, 0].astype(jnp.int32)[None], keep_count[:-1]], axis=0)
    arriving = jnp.concatenate([received[7, :, 0].astype(jnp.int32)[None], moving[:-1]], axis=0)
    distance = jnp.mod(source_keep - keep_count, slot_count)
    incoming = shift_lanes(source_field, distance)
    incoming = jnp.concatenate([incoming[:1] - 1.0, incoming[1:]], axis=0)
    slot_ids = lax.broadcasted_iota(jnp.int32, field_six.shape[1:], 2)
    own_mask = slot_ids < keep_count[..., None]
    new_mask = (slot_ids >= keep_count[..., None]) & (
        slot_ids < (keep_count + arriving)[..., None]
    )
    return jnp.where(own_mask[None], field_six, jnp.where(new_mask[None], incoming, 0.0))


def per_device(positions, velocities, plastic_viscosity, yield_stress, counts, moving):
    row_count, col_count, slot_count = positions.shape[1:]
    slot_ids = lax.broadcasted_iota(jnp.int32, (row_count, col_count, slot_count), 2)
    live = (slot_ids < counts[:, :, None]).astype(jnp.float32)
    state = jnp.concatenate([positions, velocities, live[None]], axis=0)
    state_pad = with_halo(state)
    far = jnp.where(state_pad[6:7] > 0.0, state_pad[:3], FAR_AWAY)
    sums = pair_pass(
        "density",
        jnp.concatenate([positions, velocities], axis=0),
        jnp.concatenate([far, state_pad[3:6]], axis=0),
        row_count,
        col_count,
    )
    density = PARTICLE_MASS * (KERNEL_NORM * sums[0] + KERNEL_NORM * (1.0 - live))
    strain = (PARTICLE_MASS * 20.0 * KERNEL_NORM) * sums[1]
    inverse = 1.0 / density
    pressure = STIFFNESS * (density - REST_DENSITY) * inverse * inverse
    viscosity = plastic_viscosity + yield_stress / jnp.sqrt(1.0 + strain)
    dens_pad = with_halo(jnp.stack([inverse, pressure, viscosity]))
    forces = pair_pass(
        "force",
        jnp.concatenate([positions, pressure[None], viscosity[None]], axis=0),
        jnp.concatenate([far, dens_pad[1:2], dens_pad[0:1], dens_pad[2:3]], axis=0),
        row_count,
        col_count,
    )
    scale = PARTICLE_MASS * 20.0 * KERNEL_NORM
    gravity = jnp.array([GRAVITY_DOWN, 0.0, GRAVITY_UP], jnp.float32)[:, None, None, None]
    predicted = velocities + TIME_STEP * (-scale * forces[:3] + gravity)
    diagonal = 1.0 + TIME_STEP * (scale * inverse * forces[3])
    target = jnp.concatenate([positions, viscosity[None]], axis=0)
    current = predicted
    for sweep_index in range(JACOBI):
        speed_pad = with_halo(current)
        pulled = pair_pass(
            "jacobi",
            target,
            jnp.concatenate([far, dens_pad[2:3], speed_pad * dens_pad[0:1]], axis=0),
            row_count,
            col_count,
        )
        current = (predicted + TIME_STEP * (scale * inverse * pulled)) / diagonal
    moved_positions = positions + TIME_STEP * current
    field_six = jnp.concatenate([moved_positions, current], axis=0)
    keep_count = counts - moving
    result = place_arrivals(field_six, keep_count, moving)
    return (result[:3], result[3:])


def solution(mesh):
    return jax.shard_map(
        per_device,
        mesh=mesh,
        in_specs=(
            P(None, "down", "cross", None),
            P(None, "down", "cross", None),
            P("down", "cross", None),
            P("down", "cross", None),
            P("down", "cross"),
            P("down", "cross"),
        ),
        out_specs=(P(None, "down", "cross", None), P(None, "down", "cross", None)),
        check_vma=False,
    )
```

```python
import math

import jax
import jax.numpy as jnp
from jax import lax
from jax.experimental import pallas as pl
from jax.sharding import PartitionSpec as P

MOVE_MAX = 32
JACOBI = 2


KERNEL_NORM = 21.0 / (2.0 * math.pi)
PARTICLE_MASS = 0.02
REST_DENSITY = 1.0
STIFFNESS = 2.0
TIME_STEP = 0.05
GRAVITY_DOWN = 0.5
GRAVITY_UP = -1.0
NEIGHBOUR_STEPS = [(-1, -1), (-1, 0), (-1, 1), (0, -1), (0, 0), (0, 1), (1, -1), (1, 0), (1, 1)]


def with_halo(array, sides, width):
    for axis, dim in sides:
        count, length = (lax.axis_size(axis), array.shape[dim])
        up = [(i, (i + 1) % count) for i in range(count - 1)]
        down = [(j, i) for i, j in up]
        last = lax.slice_in_dim(array, length - width, length, axis=dim)
        initial = lax.slice_in_dim(array, 0, width, axis=dim)
        before = lax.ppermute(last, axis, up)
        after = lax.ppermute(initial, axis, down)
        array = jnp.concatenate([before, array, after], axis=dim)
    return array


def from_behind(block, axis, distance):
    devices = range(lax.axis_size(axis))
    route = [(i - distance, i) for i in devices if i - distance in devices]
    return lax.ppermute(block, axis, route)


def take_row(padded, lead_blocks, row_index, step_down, step_cross, col_count):
    whole_row = lax.dynamic_index_in_dim(
        padded, row_index + lead_blocks + step_down, axis=1, keepdims=False
    )
    return whole_row[:, lead_blocks + step_cross : lead_blocks + step_cross + col_count, :]


def separation(target, source, step_down, step_cross):
    offsets = (float(step_down), float(step_cross), 0.0)
    separations = [
        source[component][:, None, :] - target[component][:, :, None] + offsets[component]
        for component in range(3)
    ]
    distance = jnp.sqrt(
        separations[0] * separations[0]
        + separations[1] * separations[1]
        + separations[2] * separations[2]
    )
    falloff = jnp.maximum(1.0 - distance, 0.0)
    falloff_cubed = falloff * falloff * falloff
    weight = KERNEL_NORM * falloff_cubed * falloff * (4.0 * distance + 1.0)
    strength = 20.0 * KERNEL_NORM * falloff_cubed
    return (separations, weight, strength)


FAR_AWAY = 1.0e4
CHUNK = 32


def pair_pass(kind, target, source, row_count, col_count):
    slot_count = target.shape[-1]
    block_count = row_count * col_count
    chunk_count = slot_count // CHUNK
    padded_cols = col_count + 2
    target_count = target.shape[0]
    source_count = source.shape[0]
    output_count = {"density": 2, "force": 4, "jacobi": 3}[kind]
    target_cols = jnp.moveaxis(target.reshape(target_count, block_count, slot_count), 0, 2)
    source_rows = source.reshape(source_count, (row_count + 2) * padded_cols, slot_count)

    def kernel(target_ref, source_ref, out_ref):
        def body(step, carry):
            block = step // chunk_count
            first = pl.multiple_of((step % chunk_count) * CHUNK, CHUNK)
            row = block // col_count
            col = block % col_count
            own = target_ref[block, pl.ds(first, CHUNK), :]
            mine = [
                jnp.broadcast_to(own[:, k : k + 1], (CHUNK, slot_count)) for k in range(target_count)
            ]
            totals = [jnp.zeros((CHUNK, slot_count), jnp.float32) for k in range(output_count)]
            for step_down, step_cross in NEIGHBOUR_STEPS:
                near = (row + 1 + step_down) * padded_cols + (col + 1 + step_cross)
                other = [source_ref[k, pl.ds(near, 1), :] for k in range(source_count)]
                gaps = [
                    other[0] + float(step_down) - mine[0],
                    other[1] + float(step_cross) - mine[1],
                    other[2] - mine[2],
                ]
                squared = gaps[0] * gaps[0] + gaps[1] * gaps[1] + gaps[2] * gaps[2]
                distance = squared * lax.rsqrt(jnp.maximum(squared, 1.0e-30))
                falloff = jnp.maximum(1.0 - distance, 0.0)
                cubed = falloff * falloff * falloff
                if kind == "density":
                    totals[0] = totals[0] + cubed * falloff * (4.0 * distance + 1.0)
                    spread = None
                    for k in range(3):
                        change = other[3 + k] - mine[3 + k]
                        term = change * change
                        spread = term if spread is None else spread + term
                    totals[1] = totals[1] + cubed * spread
                elif kind == "force":
                    push = (mine[3] + other[3]) * cubed
                    for k in range(3):
                        totals[k] = totals[k] + push * gaps[k]
                    totals[3] = totals[3] + (mine[4] + other[5]) * other[4] * cubed
                else:
                    pull = (mine[3] + other[3]) * cubed
                    for k in range(3):
                        totals[k] = totals[k] + pull * other[4 + k]
            for k in range(output_count):
                out_ref[block, pl.ds(first, CHUNK), pl.ds(k, 1)] = jnp.sum(
                    totals[k], axis=1, keepdims=True
                )
            return carry

        lax.fori_loop(0, block_count * chunk_count, body, 0)

    result = pl.pallas_call(
        kernel,
        out_shape=jax.ShapeDtypeStruct((block_count, slot_count, output_count), jnp.float32),
    )(target_cols, source_rows)
    return jnp.moveaxis(result, 2, 0).reshape(output_count, row_count, col_count, slot_count)


def shift_lanes(field, distance):
    slot_count = field.shape[-1]
    step = 1
    while step < slot_count:
        rolled = jnp.roll(field, -step, axis=-1)
        chosen = ((distance & step) != 0)[None, :, :, None]
        field = jnp.where(chosen, rolled, field)
        step *= 2
    return field


def place_arrivals(field_six, keep_count, moving):
    slot_count = field_six.shape[3]
    keep_plane = jnp.broadcast_to(keep_count[-1].astype(jnp.float32)[:, None], field_six.shape[2:])
    move_plane = jnp.broadcast_to(moving[-1].astype(jnp.float32)[:, None], field_six.shape[2:])
    edge_pack = jnp.concatenate([field_six[:, -1], keep_plane[None], move_plane[None]], axis=0)
    received = from_behind(edge_pack, "down", 1)
    source_field = jnp.concatenate([received[:6][:, None], field_six[:, :-1]], axis=1)
    source_keep = jnp.concatenate([received[6, :, 0].astype(jnp.int32)[None], keep_count[:-1]], axis=0)
    arriving = jnp.concatenate([received[7, :, 0].astype(jnp.int32)[None], moving[:-1]], axis=0)
    distance = jnp.mod(source_keep - keep_count, slot_count)
    incoming = shift_lanes(source_field, distance)
    incoming = jnp.concatenate([incoming[:1] - 1.0, incoming[1:]], axis=0)
    slot_ids = lax.broadcasted_iota(jnp.int32, field_six.shape[1:], 2)
    own_mask = slot_ids < keep_count[..., None]
    new_mask = (slot_ids >= keep_count[..., None]) & (
        slot_ids < (keep_count + arriving)[..., None]
    )
    return jnp.where(own_mask[None], field_six, jnp.where(new_mask[None], incoming, 0.0))


def per_device(positions, velocities, plastic_viscosity, yield_stress, counts, moving):
    row_count, col_count, slot_count = positions.shape[1:]
    slot_ids = lax.broadcasted_iota(jnp.int32, (row_count, col_count, slot_count), 2)
    live = (slot_ids < counts[:, :, None]).astype(jnp.float32)
    state = jnp.concatenate([positions, velocities, live[None]], axis=0)
    state_pad = with_halo(state, (("down", 1), ("cross", 2)), 1)
    far = jnp.where(state_pad[6:7] > 0.0, state_pad[:3], FAR_AWAY)
    sums = pair_pass(
        "density",
        jnp.concatenate([positions, velocities], axis=0),
        jnp.concatenate([far, state_pad[3:6]], axis=0),
        row_count,
        col_count,
    )
    density = PARTICLE_MASS * (KERNEL_NORM * sums[0] + KERNEL_NORM * (1.0 - live))
    strain = (PARTICLE_MASS * 20.0 * KERNEL_NORM) * sums[1]
    inverse = 1.0 / density
    pressure = STIFFNESS * (density - REST_DENSITY) * inverse * inverse
    viscosity = plastic_viscosity + yield_stress / jnp.sqrt(1.0 + strain)
    dens_pad = with_halo(jnp.stack([inverse, pressure, viscosity]), (("down", 1), ("cross", 2)), 1)
    forces = pair_pass(
        "force",
        jnp.concatenate([positions, pressure[None], viscosity[None]], axis=0),
        jnp.concatenate([far, dens_pad[1:2], dens_pad[0:1], dens_pad[2:3]], axis=0),
        row_count,
        col_count,
    )
    scale = PARTICLE_MASS * 20.0 * KERNEL_NORM
    gravity = jnp.array([GRAVITY_DOWN, 0.0, GRAVITY_UP], jnp.float32)[:, None, None, None]
    predicted = velocities + TIME_STEP * (-scale * forces[:3] + gravity)
    diagonal = 1.0 + TIME_STEP * (scale * inverse * forces[3])
    target = jnp.concatenate([positions, viscosity[None]], axis=0)
    current = predicted
    for sweep_index in range(JACOBI):
        speed_pad = with_halo(current, (("down", 1), ("cross", 2)), 1)
        pulled = pair_pass(
            "jacobi",
            target,
            jnp.concatenate([far, dens_pad[2:3], speed_pad * dens_pad[0:1]], axis=0),
            row_count,
            col_count,
        )
        current = (predicted + TIME_STEP * (scale * inverse * pulled)) / diagonal
    moved_positions = positions + TIME_STEP * current
    field_six = jnp.concatenate([moved_positions, current], axis=0)
    keep_count = counts - moving
    result = place_arrivals(field_six, keep_count, moving)
    return (result[:3], result[3:])


def solution(mesh):
    return jax.shard_map(
        per_device,
        mesh=mesh,
        in_specs=(
            P(None, "down", "cross", None),
            P(None, "down", "cross", None),
            P("down", "cross", None),
            P("down", "cross", None),
            P("down", "cross"),
            P("down", "cross"),
        ),
        out_specs=(P(None, "down", "cross", None), P(None, "down", "cross", None)),
        check_vma=False,
    )
```

```python
import math

import jax
import jax.numpy as jnp
from jax import lax
from jax.experimental import pallas as pl
from jax.sharding import PartitionSpec as P

MOVE_MAX = 32
JACOBI = 2


KERNEL_NORM = 21.0 / (2.0 * math.pi)
PARTICLE_MASS = 0.02
REST_DENSITY = 1.0
STIFFNESS = 2.0
TIME_STEP = 0.05
GRAVITY_DOWN = 0.5
GRAVITY_UP = -1.0
NEIGHBOUR_STEPS = [(-1, -1), (-1, 0), (-1, 1), (0, -1), (0, 0), (0, 1), (1, -1), (1, 0), (1, 1)]


def with_halo(array, sides, width):
    for axis, dim in sides:
        count, length = (lax.axis_size(axis), array.shape[dim])
        up = [(i, (i + 1) % count) for i in range(count - 1)]
        down = [(j, i) for i, j in up]
        last = lax.slice_in_dim(array, length - width, length, axis=dim)
        initial = lax.slice_in_dim(array, 0, width, axis=dim)
        before = lax.ppermute(last, axis, up)
        after = lax.ppermute(initial, axis, down)
        array = jnp.concatenate([before, array, after], axis=dim)
    return array


def from_behind(block, axis, distance):
    devices = range(lax.axis_size(axis))
    route = [(i - distance, i) for i in devices if i - distance in devices]
    return lax.ppermute(block, axis, route)


def take_row(padded, lead_blocks, row_index, step_down, step_cross, col_count):
    whole_row = lax.dynamic_index_in_dim(
        padded, row_index + lead_blocks + step_down, axis=1, keepdims=False
    )
    return whole_row[:, lead_blocks + step_cross : lead_blocks + step_cross + col_count, :]


def separation(target, source, step_down, step_cross):
    offsets = (float(step_down), float(step_cross), 0.0)
    separations = [
        source[component][:, None, :] - target[component][:, :, None] + offsets[component]
        for component in range(3)
    ]
    distance = jnp.sqrt(
        separations[0] * separations[0]
        + separations[1] * separations[1]
        + separations[2] * separations[2]
    )
    falloff = jnp.maximum(1.0 - distance, 0.0)
    falloff_cubed = falloff * falloff * falloff
    weight = KERNEL_NORM * falloff_cubed * falloff * (4.0 * distance + 1.0)
    strength = 20.0 * KERNEL_NORM * falloff_cubed
    return (separations, weight, strength)


FAR_AWAY = 1.0e4
CHUNK = 32


def pair_pass(kind, target, source, row_count, col_count, weights=None):
    slot_count = target.shape[-1]
    block_count = row_count * col_count
    chunk_count = slot_count // CHUNK
    padded_cols = col_count + 2
    target_count = target.shape[0]
    source_count = source.shape[0]
    output_count = {"density": 2, "force": 4, "jacobi": 3}[kind]
    target_cols = jnp.moveaxis(target.reshape(target_count, block_count, slot_count), 0, 2)
    source_rows = source.reshape(source_count, (row_count + 2) * padded_cols, slot_count)

    def kernel(target_ref, source_ref, *refs):
        if kind == "force":
            out_ref, weight_ref = refs
        elif kind == "jacobi":
            weight_ref, out_ref = refs
        else:
            (out_ref,) = refs

        def body(step, carry):
            block = step // chunk_count
            first = pl.multiple_of((step % chunk_count) * CHUNK, CHUNK)
            row = block // col_count
            col = block % col_count
            own = target_ref[block, pl.ds(first, CHUNK), :]
            mine = [
                jnp.broadcast_to(own[:, k : k + 1], (CHUNK, slot_count)) for k in range(target_count)
            ]
            totals = [jnp.zeros((CHUNK, slot_count), jnp.float32) for k in range(output_count)]
            for neighbour, (step_down, step_cross) in enumerate(NEIGHBOUR_STEPS):
                near = (row + 1 + step_down) * padded_cols + (col + 1 + step_cross)
                other = [source_ref[k, pl.ds(near, 1), :] for k in range(source_count)]
                if kind == "jacobi":
                    pull = weight_ref[step * 9 + neighbour]
                    for k in range(3):
                        totals[k] = totals[k] + pull * other[k]
                    continue
                gaps = [
                    other[0] + float(step_down) - mine[0],
                    other[1] + float(step_cross) - mine[1],
                    other[2] - mine[2],
                ]
                squared = gaps[0] * gaps[0] + gaps[1] * gaps[1] + gaps[2] * gaps[2]
                distance = squared * lax.rsqrt(jnp.maximum(squared, 1.0e-30))
                falloff = jnp.maximum(1.0 - distance, 0.0)
                cubed = falloff * falloff * falloff
                if kind == "density":
                    totals[0] = totals[0] + cubed * falloff * (4.0 * distance + 1.0)
                    spread = None
                    for k in range(3):
                        change = other[3 + k] - mine[3 + k]
                        term = change * change
                        spread = term if spread is None else spread + term
                    totals[1] = totals[1] + cubed * spread
                elif kind == "force":
                    push = (mine[3] + other[3]) * cubed
                    for k in range(3):
                        totals[k] = totals[k] + push * gaps[k]
                    pull = (mine[4] + other[5]) * cubed
                    weight_ref[step * 9 + neighbour] = pull
                    totals[3] = totals[3] + pull * other[4]
            for k in range(output_count):
                out_ref[block, pl.ds(first, CHUNK), pl.ds(k, 1)] = jnp.sum(
                    totals[k], axis=1, keepdims=True
                )
            return carry

        lax.fori_loop(0, block_count * chunk_count, body, 0)

    out_shape = jax.ShapeDtypeStruct((block_count, slot_count, output_count), jnp.float32)
    if kind == "force":
        weight_shape = jax.ShapeDtypeStruct(
            (block_count * chunk_count * 9, CHUNK, slot_count), jnp.float32
        )
        result, weights = pl.pallas_call(kernel, out_shape=(out_shape, weight_shape))(
            target_cols, source_rows
        )
    elif kind == "jacobi":
        result = pl.pallas_call(kernel, out_shape=out_shape)(target_cols, source_rows, weights)
    else:
        result = pl.pallas_call(kernel, out_shape=out_shape)(target_cols, source_rows)
    result = jnp.moveaxis(result, 2, 0).reshape(output_count, row_count, col_count, slot_count)
    if kind == "force":
        return result, weights
    return result


def shift_lanes(field, distance):
    slot_count = field.shape[-1]
    step = 1
    while step < slot_count:
        rolled = jnp.roll(field, -step, axis=-1)
        chosen = ((distance & step) != 0)[None, :, :, None]
        field = jnp.where(chosen, rolled, field)
        step *= 2
    return field


def place_arrivals(field_six, keep_count, moving):
    slot_count = field_six.shape[3]
    keep_plane = jnp.broadcast_to(keep_count[-1].astype(jnp.float32)[:, None], field_six.shape[2:])
    move_plane = jnp.broadcast_to(moving[-1].astype(jnp.float32)[:, None], field_six.shape[2:])
    edge_pack = jnp.concatenate([field_six[:, -1], keep_plane[None], move_plane[None]], axis=0)
    received = from_behind(edge_pack, "down", 1)
    source_field = jnp.concatenate([received[:6][:, None], field_six[:, :-1]], axis=1)
    source_keep = jnp.concatenate([received[6, :, 0].astype(jnp.int32)[None], keep_count[:-1]], axis=0)
    arriving = jnp.concatenate([received[7, :, 0].astype(jnp.int32)[None], moving[:-1]], axis=0)
    distance = jnp.mod(source_keep - keep_count, slot_count)
    incoming = shift_lanes(source_field, distance)
    incoming = jnp.concatenate([incoming[:1] - 1.0, incoming[1:]], axis=0)
    slot_ids = lax.broadcasted_iota(jnp.int32, field_six.shape[1:], 2)
    own_mask = slot_ids < keep_count[..., None]
    new_mask = (slot_ids >= keep_count[..., None]) & (
        slot_ids < (keep_count + arriving)[..., None]
    )
    return jnp.where(own_mask[None], field_six, jnp.where(new_mask[None], incoming, 0.0))


def per_device(positions, velocities, plastic_viscosity, yield_stress, counts, moving):
    row_count, col_count, slot_count = positions.shape[1:]
    slot_ids = lax.broadcasted_iota(jnp.int32, (row_count, col_count, slot_count), 2)
    live = (slot_ids < counts[:, :, None]).astype(jnp.float32)
    state = jnp.concatenate([positions, velocities, live[None]], axis=0)
    state_pad = with_halo(state, (("down", 1), ("cross", 2)), 1)
    far = jnp.where(state_pad[6:7] > 0.0, state_pad[:3], FAR_AWAY)
    sums = pair_pass(
        "density",
        jnp.concatenate([positions, velocities], axis=0),
        jnp.concatenate([far, state_pad[3:6]], axis=0),
        row_count,
        col_count,
    )
    density = PARTICLE_MASS * (KERNEL_NORM * sums[0] + KERNEL_NORM * (1.0 - live))
    strain = (PARTICLE_MASS * 20.0 * KERNEL_NORM) * sums[1]
    inverse = 1.0 / density
    pressure = STIFFNESS * (density - REST_DENSITY) * inverse * inverse
    viscosity = plastic_viscosity + yield_stress / jnp.sqrt(1.0 + strain)
    dens_pad = with_halo(jnp.stack([inverse, pressure, viscosity]), (("down", 1), ("cross", 2)), 1)
    forces, weights = pair_pass(
        "force",
        jnp.concatenate([positions, pressure[None], viscosity[None]], axis=0),
        jnp.concatenate([far, dens_pad[1:2], dens_pad[0:1], dens_pad[2:3]], axis=0),
        row_count,
        col_count,
    )
    scale = PARTICLE_MASS * 20.0 * KERNEL_NORM
    gravity = jnp.array([GRAVITY_DOWN, 0.0, GRAVITY_UP], jnp.float32)[:, None, None, None]
    predicted = velocities + TIME_STEP * (-scale * forces[:3] + gravity)
    diagonal = 1.0 + TIME_STEP * (scale * inverse * forces[3])
    target = jnp.concatenate([positions, viscosity[None]], axis=0)
    current = predicted
    for sweep_index in range(JACOBI):
        speed_pad = with_halo(current, (("down", 1), ("cross", 2)), 1)
        pulled = pair_pass(
            "jacobi",
            target,
            speed_pad * dens_pad[0:1],
            row_count,
            col_count,
            weights,
        )
        current = (predicted + TIME_STEP * (scale * inverse * pulled)) / diagonal
    moved_positions = positions + TIME_STEP * current
    field_six = jnp.concatenate([moved_positions, current], axis=0)
    keep_count = counts - moving
    result = place_arrivals(field_six, keep_count, moving)
    return (result[:3], result[3:])


def solution(mesh):
    return jax.shard_map(
        per_device,
        mesh=mesh,
        in_specs=(
            P(None, "down", "cross", None),
            P(None, "down", "cross", None),
            P("down", "cross", None),
            P("down", "cross", None),
            P("down", "cross"),
            P("down", "cross"),
        ),
        out_specs=(P(None, "down", "cross", None), P(None, "down", "cross", None)),
        check_vma=False,
    )
```

```python
import math

import jax
import jax.numpy as jnp
from jax import lax
from jax.experimental import pallas as pl
from jax.sharding import PartitionSpec as P

MOVE_MAX = 32
JACOBI = 2


KERNEL_NORM = 21.0 / (2.0 * math.pi)
PARTICLE_MASS = 0.02
REST_DENSITY = 1.0
STIFFNESS = 2.0
TIME_STEP = 0.05
GRAVITY_DOWN = 0.5
GRAVITY_UP = -1.0
NEIGHBOUR_STEPS = [(-1, -1), (-1, 0), (-1, 1), (0, -1), (0, 0), (0, 1), (1, -1), (1, 0), (1, 1)]


def with_halo(array, sides, width):
    for axis, dim in sides:
        count, length = (lax.axis_size(axis), array.shape[dim])
        up = [(i, (i + 1) % count) for i in range(count - 1)]
        down = [(j, i) for i, j in up]
        last = lax.slice_in_dim(array, length - width, length, axis=dim)
        initial = lax.slice_in_dim(array, 0, width, axis=dim)
        before = lax.ppermute(last, axis, up)
        after = lax.ppermute(initial, axis, down)
        array = jnp.concatenate([before, array, after], axis=dim)
    return array


def from_behind(block, axis, distance):
    devices = range(lax.axis_size(axis))
    route = [(i - distance, i) for i in devices if i - distance in devices]
    return lax.ppermute(block, axis, route)


def take_row(padded, lead_blocks, row_index, step_down, step_cross, col_count):
    whole_row = lax.dynamic_index_in_dim(
        padded, row_index + lead_blocks + step_down, axis=1, keepdims=False
    )
    return whole_row[:, lead_blocks + step_cross : lead_blocks + step_cross + col_count, :]


def separation(target, source, step_down, step_cross):
    offsets = (float(step_down), float(step_cross), 0.0)
    separations = [
        source[component][:, None, :] - target[component][:, :, None] + offsets[component]
        for component in range(3)
    ]
    distance = jnp.sqrt(
        separations[0] * separations[0]
        + separations[1] * separations[1]
        + separations[2] * separations[2]
    )
    falloff = jnp.maximum(1.0 - distance, 0.0)
    falloff_cubed = falloff * falloff * falloff
    weight = KERNEL_NORM * falloff_cubed * falloff * (4.0 * distance + 1.0)
    strength = 20.0 * KERNEL_NORM * falloff_cubed
    return (separations, weight, strength)


FAR_AWAY = 1.0e4
CHUNK = 32


def pair_pass(kind, target, source, row_count, col_count, weights=None):
    slot_count = target.shape[-1]
    block_count = row_count * col_count
    chunk_count = slot_count // CHUNK
    padded_cols = col_count + 2
    target_count = target.shape[0]
    source_count = source.shape[0]
    output_count = {"density": 2, "force": 4, "jacobi": 3}[kind]
    target_cols = jnp.moveaxis(target.reshape(target_count, block_count, slot_count), 0, 2)
    source_rows = source.reshape(source_count, (row_count + 2) * padded_cols, slot_count)

    def kernel(target_ref, source_ref, *refs):
        if kind == "force":
            out_ref, weight_ref = refs
        elif kind == "jacobi":
            weight_ref, out_ref = refs
        else:
            (out_ref,) = refs

        block = pl.program_id(0)

        def body(step, carry):
            first = pl.multiple_of(step * CHUNK, CHUNK)
            row = block // col_count
            col = block % col_count
            own = target_ref[block, pl.ds(first, CHUNK), :]
            mine = [
                jnp.broadcast_to(own[:, k : k + 1], (CHUNK, slot_count)) for k in range(target_count)
            ]
            totals = [jnp.zeros((CHUNK, slot_count), jnp.float32) for k in range(output_count)]
            for neighbour, (step_down, step_cross) in enumerate(NEIGHBOUR_STEPS):
                near = (row + 1 + step_down) * padded_cols + (col + 1 + step_cross)
                other = [source_ref[k, pl.ds(near, 1), :] for k in range(source_count)]
                if kind == "jacobi":
                    pull = weight_ref[step * 9 + neighbour]
                    for k in range(3):
                        totals[k] = totals[k] + pull * other[k]
                    continue
                gaps = [
                    other[0] + float(step_down) - mine[0],
                    other[1] + float(step_cross) - mine[1],
                    other[2] - mine[2],
                ]
                squared = gaps[0] * gaps[0] + gaps[1] * gaps[1] + gaps[2] * gaps[2]
                distance = squared * lax.rsqrt(jnp.maximum(squared, 1.0e-30))
                falloff = jnp.maximum(1.0 - distance, 0.0)
                cubed = falloff * falloff * falloff
                if kind == "density":
                    totals[0] = totals[0] + cubed * falloff * (4.0 * distance + 1.0)
                    spread = None
                    for k in range(3):
                        change = other[3 + k] - mine[3 + k]
                        term = change * change
                        spread = term if spread is None else spread + term
                    totals[1] = totals[1] + cubed * spread
                elif kind == "force":
                    push = (mine[3] + other[3]) * cubed
                    for k in range(3):
                        totals[k] = totals[k] + push * gaps[k]
                    pull = (mine[4] + other[5]) * cubed
                    weight_ref[step * 9 + neighbour] = pull
                    totals[3] = totals[3] + pull * other[4]
            for k in range(output_count):
                out_ref[block, pl.ds(first, CHUNK), pl.ds(k, 1)] = jnp.sum(
                    totals[k], axis=1, keepdims=True
                )
            return carry

        lax.fori_loop(0, chunk_count, body, 0)

    out_shape = jax.ShapeDtypeStruct((block_count, slot_count, output_count), jnp.float32)
    whole = [
        pl.BlockSpec(target_cols.shape, lambda block: (0, 0, 0)),
        pl.BlockSpec(source_rows.shape, lambda block: (0, 0, 0)),
    ]
    out_spec = pl.BlockSpec(out_shape.shape, lambda block: (0, 0, 0))
    weight_spec = pl.BlockSpec((chunk_count * 9, CHUNK, slot_count), lambda block: (block, 0, 0))
    grid = (block_count,)
    if kind == "force":
        weight_shape = jax.ShapeDtypeStruct(
            (block_count * chunk_count * 9, CHUNK, slot_count), jnp.float32
        )
        result, weights = pl.pallas_call(
            kernel,
            out_shape=(out_shape, weight_shape),
            grid=grid,
            in_specs=whole,
            out_specs=(out_spec, weight_spec),
        )(target_cols, source_rows)
    elif kind == "jacobi":
        result = pl.pallas_call(
            kernel,
            out_shape=out_shape,
            grid=grid,
            in_specs=whole + [weight_spec],
            out_specs=out_spec,
        )(target_cols, source_rows, weights)
    else:
        result = pl.pallas_call(
            kernel, out_shape=out_shape, grid=grid, in_specs=whole, out_specs=out_spec
        )(target_cols, source_rows)
    result = jnp.moveaxis(result, 2, 0).reshape(output_count, row_count, col_count, slot_count)
    if kind == "force":
        return result, weights
    return result


def shift_lanes(field, distance):
    slot_count = field.shape[-1]
    step = 1
    while step < slot_count:
        rolled = jnp.roll(field, -step, axis=-1)
        chosen = ((distance & step) != 0)[None, :, :, None]
        field = jnp.where(chosen, rolled, field)
        step *= 2
    return field


def place_arrivals(field_six, keep_count, moving):
    slot_count = field_six.shape[3]
    keep_plane = jnp.broadcast_to(keep_count[-1].astype(jnp.float32)[:, None], field_six.shape[2:])
    move_plane = jnp.broadcast_to(moving[-1].astype(jnp.float32)[:, None], field_six.shape[2:])
    edge_pack = jnp.concatenate([field_six[:, -1], keep_plane[None], move_plane[None]], axis=0)
    received = from_behind(edge_pack, "down", 1)
    source_field = jnp.concatenate([received[:6][:, None], field_six[:, :-1]], axis=1)
    source_keep = jnp.concatenate([received[6, :, 0].astype(jnp.int32)[None], keep_count[:-1]], axis=0)
    arriving = jnp.concatenate([received[7, :, 0].astype(jnp.int32)[None], moving[:-1]], axis=0)
    distance = jnp.mod(source_keep - keep_count, slot_count)
    incoming = shift_lanes(source_field, distance)
    incoming = jnp.concatenate([incoming[:1] - 1.0, incoming[1:]], axis=0)
    slot_ids = lax.broadcasted_iota(jnp.int32, field_six.shape[1:], 2)
    own_mask = slot_ids < keep_count[..., None]
    new_mask = (slot_ids >= keep_count[..., None]) & (
        slot_ids < (keep_count + arriving)[..., None]
    )
    return jnp.where(own_mask[None], field_six, jnp.where(new_mask[None], incoming, 0.0))


def per_device(positions, velocities, plastic_viscosity, yield_stress, counts, moving):
    row_count, col_count, slot_count = positions.shape[1:]
    slot_ids = lax.broadcasted_iota(jnp.int32, (row_count, col_count, slot_count), 2)
    live = (slot_ids < counts[:, :, None]).astype(jnp.float32)
    state = jnp.concatenate([positions, velocities, live[None]], axis=0)
    state_pad = with_halo(state, (("down", 1), ("cross", 2)), 1)
    far = jnp.where(state_pad[6:7] > 0.0, state_pad[:3], FAR_AWAY)
    sums = pair_pass(
        "density",
        jnp.concatenate([positions, velocities], axis=0),
        jnp.concatenate([far, state_pad[3:6]], axis=0),
        row_count,
        col_count,
    )
    density = PARTICLE_MASS * (KERNEL_NORM * sums[0] + KERNEL_NORM * (1.0 - live))
    strain = (PARTICLE_MASS * 20.0 * KERNEL_NORM) * sums[1]
    inverse = 1.0 / density
    pressure = STIFFNESS * (density - REST_DENSITY) * inverse * inverse
    viscosity = plastic_viscosity + yield_stress / jnp.sqrt(1.0 + strain)
    dens_pad = with_halo(jnp.stack([inverse, pressure, viscosity]), (("down", 1), ("cross", 2)), 1)
    forces, weights = pair_pass(
        "force",
        jnp.concatenate([positions, pressure[None], viscosity[None]], axis=0),
        jnp.concatenate([far, dens_pad[1:2], dens_pad[0:1], dens_pad[2:3]], axis=0),
        row_count,
        col_count,
    )
    scale = PARTICLE_MASS * 20.0 * KERNEL_NORM
    gravity = jnp.array([GRAVITY_DOWN, 0.0, GRAVITY_UP], jnp.float32)[:, None, None, None]
    predicted = velocities + TIME_STEP * (-scale * forces[:3] + gravity)
    diagonal = 1.0 + TIME_STEP * (scale * inverse * forces[3])
    target = jnp.concatenate([positions, viscosity[None]], axis=0)
    current = predicted
    for sweep_index in range(JACOBI):
        speed_pad = with_halo(current, (("down", 1), ("cross", 2)), 1)
        pulled = pair_pass(
            "jacobi",
            target,
            speed_pad * dens_pad[0:1],
            row_count,
            col_count,
            weights,
        )
        current = (predicted + TIME_STEP * (scale * inverse * pulled)) / diagonal
    moved_positions = positions + TIME_STEP * current
    field_six = jnp.concatenate([moved_positions, current], axis=0)
    keep_count = counts - moving
    result = place_arrivals(field_six, keep_count, moving)
    return (result[:3], result[3:])


def solution(mesh):
    return jax.shard_map(
        per_device,
        mesh=mesh,
        in_specs=(
            P(None, "down", "cross", None),
            P(None, "down", "cross", None),
            P("down", "cross", None),
            P("down", "cross", None),
            P("down", "cross"),
            P("down", "cross"),
        ),
        out_specs=(P(None, "down", "cross", None), P(None, "down", "cross", None)),
        check_vma=False,
    )
```

```python
import math

import jax
import jax.numpy as jnp
from jax import lax
from jax.experimental import pallas as pl
from jax.sharding import PartitionSpec as P

MOVE_MAX = 32
JACOBI = 2


KERNEL_NORM = 21.0 / (2.0 * math.pi)
PARTICLE_MASS = 0.02
REST_DENSITY = 1.0
STIFFNESS = 2.0
TIME_STEP = 0.05
GRAVITY_DOWN = 0.5
GRAVITY_UP = -1.0
NEIGHBOUR_STEPS = [(-1, -1), (-1, 0), (-1, 1), (0, -1), (0, 0), (0, 1), (1, -1), (1, 0), (1, 1)]


def with_halo(array, sides, width):
    for axis, dim in sides:
        count, length = (lax.axis_size(axis), array.shape[dim])
        up = [(i, (i + 1) % count) for i in range(count - 1)]
        down = [(j, i) for i, j in up]
        last = lax.slice_in_dim(array, length - width, length, axis=dim)
        initial = lax.slice_in_dim(array, 0, width, axis=dim)
        before = lax.ppermute(last, axis, up)
        after = lax.ppermute(initial, axis, down)
        array = jnp.concatenate([before, array, after], axis=dim)
    return array


def from_behind(block, axis, distance):
    devices = range(lax.axis_size(axis))
    route = [(i - distance, i) for i in devices if i - distance in devices]
    return lax.ppermute(block, axis, route)


def take_row(padded, lead_blocks, row_index, step_down, step_cross, col_count):
    whole_row = lax.dynamic_index_in_dim(
        padded, row_index + lead_blocks + step_down, axis=1, keepdims=False
    )
    return whole_row[:, lead_blocks + step_cross : lead_blocks + step_cross + col_count, :]


def separation(target, source, step_down, step_cross):
    offsets = (float(step_down), float(step_cross), 0.0)
    separations = [
        source[component][:, None, :] - target[component][:, :, None] + offsets[component]
        for component in range(3)
    ]
    distance = jnp.sqrt(
        separations[0] * separations[0]
        + separations[1] * separations[1]
        + separations[2] * separations[2]
    )
    falloff = jnp.maximum(1.0 - distance, 0.0)
    falloff_cubed = falloff * falloff * falloff
    weight = KERNEL_NORM * falloff_cubed * falloff * (4.0 * distance + 1.0)
    strength = 20.0 * KERNEL_NORM * falloff_cubed
    return (separations, weight, strength)


FAR_AWAY = 1.0e4
CHUNK = 32


def pair_pass(kind, target, source, row_count, col_count, weights=None):
    slot_count = target.shape[-1]
    block_count = row_count * col_count
    chunk_count = slot_count // CHUNK
    padded_cols = col_count + 2
    target_count = target.shape[0]
    source_count = source.shape[0]
    output_count = {"density": 2, "force": 4, "jacobi": 3}[kind]
    target_cols = jnp.moveaxis(target.reshape(target_count, block_count, slot_count), 0, 2)
    source_rows = source.reshape(source_count, (row_count + 2) * padded_cols, slot_count)

    def kernel(target_ref, source_ref, *refs):
        if kind == "force":
            out_ref, weight_ref = refs
        elif kind == "jacobi":
            weight_ref, out_ref = refs
        else:
            (out_ref,) = refs

        grid_block = None if kind == "jacobi" else pl.program_id(0)

        def body(step, carry):
            if kind == "jacobi":
                block = step // chunk_count
                first = pl.multiple_of((step % chunk_count) * CHUNK, CHUNK)
            else:
                block = grid_block
                first = pl.multiple_of(step * CHUNK, CHUNK)
            row = block // col_count
            col = block % col_count
            own = target_ref[block, pl.ds(first, CHUNK), :]
            mine = [
                jnp.broadcast_to(own[:, k : k + 1], (CHUNK, slot_count)) for k in range(target_count)
            ]
            totals = [jnp.zeros((CHUNK, slot_count), jnp.float32) for k in range(output_count)]
            for neighbour, (step_down, step_cross) in enumerate(NEIGHBOUR_STEPS):
                near = (row + 1 + step_down) * padded_cols + (col + 1 + step_cross)
                other = [source_ref[k, pl.ds(near, 1), :] for k in range(source_count)]
                if kind == "jacobi":
                    pull = weight_ref[step * 9 + neighbour]
                    for k in range(3):
                        totals[k] = totals[k] + pull * other[k]
                    continue
                gaps = [
                    other[0] + float(step_down) - mine[0],
                    other[1] + float(step_cross) - mine[1],
                    other[2] - mine[2],
                ]
                squared = gaps[0] * gaps[0] + gaps[1] * gaps[1] + gaps[2] * gaps[2]
                distance = squared * lax.rsqrt(jnp.maximum(squared, 1.0e-30))
                falloff = jnp.maximum(1.0 - distance, 0.0)
                cubed = falloff * falloff * falloff
                if kind == "density":
                    totals[0] = totals[0] + cubed * falloff * (4.0 * distance + 1.0)
                    spread = None
                    for k in range(3):
                        change = other[3 + k] - mine[3 + k]
                        term = change * change
                        spread = term if spread is None else spread + term
                    totals[1] = totals[1] + cubed * spread
                elif kind == "force":
                    push = (mine[3] + other[3]) * cubed
                    for k in range(3):
                        totals[k] = totals[k] + push * gaps[k]
                    pull = (mine[4] + other[5]) * cubed
                    weight_ref[step * 9 + neighbour] = pull
                    totals[3] = totals[3] + pull * other[4]
            for k in range(output_count):
                out_ref[block, pl.ds(first, CHUNK), pl.ds(k, 1)] = jnp.sum(
                    totals[k], axis=1, keepdims=True
                )
            return carry

        lax.fori_loop(0, block_count * chunk_count if kind == "jacobi" else chunk_count, body, 0)

    out_shape = jax.ShapeDtypeStruct((block_count, slot_count, output_count), jnp.float32)
    whole = [
        pl.BlockSpec(target_cols.shape, lambda block: (0, 0, 0)),
        pl.BlockSpec(source_rows.shape, lambda block: (0, 0, 0)),
    ]
    out_spec = pl.BlockSpec(out_shape.shape, lambda block: (0, 0, 0))
    weight_spec = pl.BlockSpec((chunk_count * 9, CHUNK, slot_count), lambda block: (block, 0, 0))
    grid = (block_count,)
    if kind == "force":
        weight_shape = jax.ShapeDtypeStruct(
            (block_count * chunk_count * 9, CHUNK, slot_count), jnp.float32
        )
        result, weights = pl.pallas_call(
            kernel,
            out_shape=(out_shape, weight_shape),
            grid=grid,
            in_specs=whole,
            out_specs=(out_spec, weight_spec),
        )(target_cols, source_rows)
    elif kind == "jacobi":
        result = pl.pallas_call(kernel, out_shape=out_shape)(target_cols, source_rows, weights)
    else:
        result = pl.pallas_call(
            kernel, out_shape=out_shape, grid=grid, in_specs=whole, out_specs=out_spec
        )(target_cols, source_rows)
    result = jnp.moveaxis(result, 2, 0).reshape(output_count, row_count, col_count, slot_count)
    if kind == "force":
        return result, weights
    return result


def shift_lanes(field, distance):
    slot_count = field.shape[-1]
    step = 1
    while step < slot_count:
        rolled = jnp.roll(field, -step, axis=-1)
        chosen = ((distance & step) != 0)[None, :, :, None]
        field = jnp.where(chosen, rolled, field)
        step *= 2
    return field


def place_arrivals(field_six, keep_count, moving):
    slot_count = field_six.shape[3]
    keep_plane = jnp.broadcast_to(keep_count[-1].astype(jnp.float32)[:, None], field_six.shape[2:])
    move_plane = jnp.broadcast_to(moving[-1].astype(jnp.float32)[:, None], field_six.shape[2:])
    edge_pack = jnp.concatenate([field_six[:, -1], keep_plane[None], move_plane[None]], axis=0)
    received = from_behind(edge_pack, "down", 1)
    source_field = jnp.concatenate([received[:6][:, None], field_six[:, :-1]], axis=1)
    source_keep = jnp.concatenate([received[6, :, 0].astype(jnp.int32)[None], keep_count[:-1]], axis=0)
    arriving = jnp.concatenate([received[7, :, 0].astype(jnp.int32)[None], moving[:-1]], axis=0)
    distance = jnp.mod(source_keep - keep_count, slot_count)
    incoming = shift_lanes(source_field, distance)
    incoming = jnp.concatenate([incoming[:1] - 1.0, incoming[1:]], axis=0)
    slot_ids = lax.broadcasted_iota(jnp.int32, field_six.shape[1:], 2)
    own_mask = slot_ids < keep_count[..., None]
    new_mask = (slot_ids >= keep_count[..., None]) & (
        slot_ids < (keep_count + arriving)[..., None]
    )
    return jnp.where(own_mask[None], field_six, jnp.where(new_mask[None], incoming, 0.0))


def per_device(positions, velocities, plastic_viscosity, yield_stress, counts, moving):
    row_count, col_count, slot_count = positions.shape[1:]
    slot_ids = lax.broadcasted_iota(jnp.int32, (row_count, col_count, slot_count), 2)
    live = (slot_ids < counts[:, :, None]).astype(jnp.float32)
    state = jnp.concatenate([positions, velocities, live[None]], axis=0)
    state_pad = with_halo(state, (("down", 1), ("cross", 2)), 1)
    far = jnp.where(state_pad[6:7] > 0.0, state_pad[:3], FAR_AWAY)
    sums = pair_pass(
        "density",
        jnp.concatenate([positions, velocities], axis=0),
        jnp.concatenate([far, state_pad[3:6]], axis=0),
        row_count,
        col_count,
    )
    density = PARTICLE_MASS * (KERNEL_NORM * sums[0] + KERNEL_NORM * (1.0 - live))
    strain = (PARTICLE_MASS * 20.0 * KERNEL_NORM) * sums[1]
    inverse = 1.0 / density
    pressure = STIFFNESS * (density - REST_DENSITY) * inverse * inverse
    viscosity = plastic_viscosity + yield_stress / jnp.sqrt(1.0 + strain)
    dens_pad = with_halo(jnp.stack([inverse, pressure, viscosity]), (("down", 1), ("cross", 2)), 1)
    forces, weights = pair_pass(
        "force",
        jnp.concatenate([positions, pressure[None], viscosity[None]], axis=0),
        jnp.concatenate([far, dens_pad[1:2], dens_pad[0:1], dens_pad[2:3]], axis=0),
        row_count,
        col_count,
    )
    scale = PARTICLE_MASS * 20.0 * KERNEL_NORM
    gravity = jnp.array([GRAVITY_DOWN, 0.0, GRAVITY_UP], jnp.float32)[:, None, None, None]
    predicted = velocities + TIME_STEP * (-scale * forces[:3] + gravity)
    diagonal = 1.0 + TIME_STEP * (scale * inverse * forces[3])
    target = viscosity[None]
    current = predicted
    for sweep_index in range(JACOBI):
        speed_pad = with_halo(current, (("down", 1), ("cross", 2)), 1)
        pulled = pair_pass(
            "jacobi",
            target,
            speed_pad * dens_pad[0:1],
            row_count,
            col_count,
            weights,
        )
        current = (predicted + TIME_STEP * (scale * inverse * pulled)) / diagonal
    moved_positions = positions + TIME_STEP * current
    field_six = jnp.concatenate([moved_positions, current], axis=0)
    keep_count = counts - moving
    result = place_arrivals(field_six, keep_count, moving)
    return (result[:3], result[3:])


def solution(mesh):
    return jax.shard_map(
        per_device,
        mesh=mesh,
        in_specs=(
            P(None, "down", "cross", None),
            P(None, "down", "cross", None),
            P("down", "cross", None),
            P("down", "cross", None),
            P("down", "cross"),
            P("down", "cross"),
        ),
        out_specs=(P(None, "down", "cross", None), P(None, "down", "cross", None)),
        check_vma=False,
    )
```

```python
import math

import jax
import jax.numpy as jnp
from jax import lax
from jax.experimental import pallas as pl
from jax.sharding import PartitionSpec as P

MOVE_MAX = 32
JACOBI = 2


KERNEL_NORM = 21.0 / (2.0 * math.pi)
PARTICLE_MASS = 0.02
REST_DENSITY = 1.0
STIFFNESS = 2.0
TIME_STEP = 0.05
GRAVITY_DOWN = 0.5
GRAVITY_UP = -1.0
NEIGHBOUR_STEPS = [(-1, -1), (-1, 0), (-1, 1), (0, -1), (0, 0), (0, 1), (1, -1), (1, 0), (1, 1)]


def with_halo(array, sides, width):
    for axis, dim in sides:
        count, length = (lax.axis_size(axis), array.shape[dim])
        up = [(i, (i + 1) % count) for i in range(count - 1)]
        down = [(j, i) for i, j in up]
        last = lax.slice_in_dim(array, length - width, length, axis=dim)
        initial = lax.slice_in_dim(array, 0, width, axis=dim)
        before = lax.ppermute(last, axis, up)
        after = lax.ppermute(initial, axis, down)
        array = jnp.concatenate([before, array, after], axis=dim)
    return array


def from_behind(block, axis, distance):
    devices = range(lax.axis_size(axis))
    route = [(i - distance, i) for i in devices if i - distance in devices]
    return lax.ppermute(block, axis, route)


def take_row(padded, lead_blocks, row_index, step_down, step_cross, col_count):
    whole_row = lax.dynamic_index_in_dim(
        padded, row_index + lead_blocks + step_down, axis=1, keepdims=False
    )
    return whole_row[:, lead_blocks + step_cross : lead_blocks + step_cross + col_count, :]


def separation(target, source, step_down, step_cross):
    offsets = (float(step_down), float(step_cross), 0.0)
    separations = [
        source[component][:, None, :] - target[component][:, :, None] + offsets[component]
        for component in range(3)
    ]
    distance = jnp.sqrt(
        separations[0] * separations[0]
        + separations[1] * separations[1]
        + separations[2] * separations[2]
    )
    falloff = jnp.maximum(1.0 - distance, 0.0)
    falloff_cubed = falloff * falloff * falloff
    weight = KERNEL_NORM * falloff_cubed * falloff * (4.0 * distance + 1.0)
    strength = 20.0 * KERNEL_NORM * falloff_cubed
    return (separations, weight, strength)


FAR_AWAY = 1.0e4
CHUNK = 128


def pair_pass(kind, target, source, row_count, col_count, weights=None):
    slot_count = target.shape[-1]
    block_count = row_count * col_count
    chunk_count = slot_count // CHUNK
    padded_cols = col_count + 2
    target_count = target.shape[0]
    source_count = source.shape[0]
    output_count = {"density": 2, "force": 4, "jacobi": 3}[kind]
    target_cols = jnp.moveaxis(target.reshape(target_count, block_count, slot_count), 0, 2)
    source_rows = source.reshape(source_count, (row_count + 2) * padded_cols, slot_count)

    def kernel(target_ref, source_ref, *refs):
        if kind == "force":
            out_ref, weight_ref = refs
        elif kind == "jacobi":
            weight_ref, out_ref = refs
        else:
            (out_ref,) = refs

        grid_block = None if kind == "jacobi" else pl.program_id(0)

        def body(step, carry):
            if kind == "jacobi":
                block = step // chunk_count
                first = pl.multiple_of((step % chunk_count) * CHUNK, CHUNK)
            else:
                block = grid_block
                first = pl.multiple_of(step * CHUNK, CHUNK)
            row = block // col_count
            col = block % col_count
            own = target_ref[block, pl.ds(first, CHUNK), :]
            mine = [
                jnp.broadcast_to(own[:, k : k + 1], (CHUNK, slot_count)) for k in range(target_count)
            ]
            totals = [jnp.zeros((CHUNK, slot_count), jnp.float32) for k in range(output_count)]
            for neighbour, (step_down, step_cross) in enumerate(NEIGHBOUR_STEPS):
                near = (row + 1 + step_down) * padded_cols + (col + 1 + step_cross)
                other = [source_ref[k, pl.ds(near, 1), :] for k in range(source_count)]
                if kind == "jacobi":
                    pull = weight_ref[step * 9 + neighbour]
                    for k in range(3):
                        totals[k] = totals[k] + pull * other[k]
                    continue
                gaps = [
                    other[0] + float(step_down) - mine[0],
                    other[1] + float(step_cross) - mine[1],
                    other[2] - mine[2],
                ]
                squared = gaps[0] * gaps[0] + gaps[1] * gaps[1] + gaps[2] * gaps[2]
                distance = squared * lax.rsqrt(jnp.maximum(squared, 1.0e-30))
                falloff = jnp.maximum(1.0 - distance, 0.0)
                cubed = falloff * falloff * falloff
                if kind == "density":
                    totals[0] = totals[0] + cubed * falloff * (4.0 * distance + 1.0)
                    spread = None
                    for k in range(3):
                        change = other[3 + k] - mine[3 + k]
                        term = change * change
                        spread = term if spread is None else spread + term
                    totals[1] = totals[1] + cubed * spread
                elif kind == "force":
                    push = (mine[3] + other[3]) * cubed
                    for k in range(3):
                        totals[k] = totals[k] + push * gaps[k]
                    pull = (mine[4] + other[5]) * cubed
                    weight_ref[step * 9 + neighbour] = pull
                    totals[3] = totals[3] + pull * other[4]
            for k in range(output_count):
                out_ref[block, pl.ds(first, CHUNK), pl.ds(k, 1)] = jnp.sum(
                    totals[k], axis=1, keepdims=True
                )
            return carry

        lax.fori_loop(0, block_count * chunk_count if kind == "jacobi" else chunk_count, body, 0)

    out_shape = jax.ShapeDtypeStruct((block_count, slot_count, output_count), jnp.float32)
    whole = [
        pl.BlockSpec(target_cols.shape, lambda block: (0, 0, 0)),
        pl.BlockSpec(source_rows.shape, lambda block: (0, 0, 0)),
    ]
    out_spec = pl.BlockSpec(out_shape.shape, lambda block: (0, 0, 0))
    weight_spec = pl.BlockSpec((chunk_count * 9, CHUNK, slot_count), lambda block: (block, 0, 0))
    grid = (block_count,)
    if kind == "force":
        weight_shape = jax.ShapeDtypeStruct(
            (block_count * chunk_count * 9, CHUNK, slot_count), jnp.float32
        )
        result, weights = pl.pallas_call(
            kernel,
            out_shape=(out_shape, weight_shape),
            grid=grid,
            in_specs=whole,
            out_specs=(out_spec, weight_spec),
        )(target_cols, source_rows)
    elif kind == "jacobi":
        result = pl.pallas_call(kernel, out_shape=out_shape)(target_cols, source_rows, weights)
    else:
        result = pl.pallas_call(
            kernel, out_shape=out_shape, grid=grid, in_specs=whole, out_specs=out_spec
        )(target_cols, source_rows)
    result = jnp.moveaxis(result, 2, 0).reshape(output_count, row_count, col_count, slot_count)
    if kind == "force":
        return result, weights
    return result


def shift_lanes(field, distance):
    slot_count = field.shape[-1]
    step = 1
    while step < slot_count:
        rolled = jnp.roll(field, -step, axis=-1)
        chosen = ((distance & step) != 0)[None, :, :, None]
        field = jnp.where(chosen, rolled, field)
        step *= 2
    return field


def place_arrivals(field_six, keep_count, moving):
    slot_count = field_six.shape[3]
    keep_plane = jnp.broadcast_to(keep_count[-1].astype(jnp.float32)[:, None], field_six.shape[2:])
    move_plane = jnp.broadcast_to(moving[-1].astype(jnp.float32)[:, None], field_six.shape[2:])
    edge_pack = jnp.concatenate([field_six[:, -1], keep_plane[None], move_plane[None]], axis=0)
    received = from_behind(edge_pack, "down", 1)
    source_field = jnp.concatenate([received[:6][:, None], field_six[:, :-1]], axis=1)
    source_keep = jnp.concatenate([received[6, :, 0].astype(jnp.int32)[None], keep_count[:-1]], axis=0)
    arriving = jnp.concatenate([received[7, :, 0].astype(jnp.int32)[None], moving[:-1]], axis=0)
    distance = jnp.mod(source_keep - keep_count, slot_count)
    incoming = shift_lanes(source_field, distance)
    incoming = jnp.concatenate([incoming[:1] - 1.0, incoming[1:]], axis=0)
    slot_ids = lax.broadcasted_iota(jnp.int32, field_six.shape[1:], 2)
    own_mask = slot_ids < keep_count[..., None]
    new_mask = (slot_ids >= keep_count[..., None]) & (
        slot_ids < (keep_count + arriving)[..., None]
    )
    return jnp.where(own_mask[None], field_six, jnp.where(new_mask[None], incoming, 0.0))


def per_device(positions, velocities, plastic_viscosity, yield_stress, counts, moving):
    row_count, col_count, slot_count = positions.shape[1:]
    slot_ids = lax.broadcasted_iota(jnp.int32, (row_count, col_count, slot_count), 2)
    live = (slot_ids < counts[:, :, None]).astype(jnp.float32)
    state = jnp.concatenate([positions, velocities, live[None]], axis=0)
    state_pad = with_halo(state, (("down", 1), ("cross", 2)), 1)
    far = jnp.where(state_pad[6:7] > 0.0, state_pad[:3], FAR_AWAY)
    sums = pair_pass(
        "density",
        jnp.concatenate([positions, velocities], axis=0),
        jnp.concatenate([far, state_pad[3:6]], axis=0),
        row_count,
        col_count,
    )
    density = PARTICLE_MASS * (KERNEL_NORM * sums[0] + KERNEL_NORM * (1.0 - live))
    strain = (PARTICLE_MASS * 20.0 * KERNEL_NORM) * sums[1]
    inverse = 1.0 / density
    pressure = STIFFNESS * (density - REST_DENSITY) * inverse * inverse
    viscosity = plastic_viscosity + yield_stress / jnp.sqrt(1.0 + strain)
    dens_pad = with_halo(jnp.stack([inverse, pressure, viscosity]), (("down", 1), ("cross", 2)), 1)
    forces, weights = pair_pass(
        "force",
        jnp.concatenate([positions, pressure[None], viscosity[None]], axis=0),
        jnp.concatenate([far, dens_pad[1:2], dens_pad[0:1], dens_pad[2:3]], axis=0),
        row_count,
        col_count,
    )
    scale = PARTICLE_MASS * 20.0 * KERNEL_NORM
    gravity = jnp.array([GRAVITY_DOWN, 0.0, GRAVITY_UP], jnp.float32)[:, None, None, None]
    predicted = velocities + TIME_STEP * (-scale * forces[:3] + gravity)
    diagonal = 1.0 + TIME_STEP * (scale * inverse * forces[3])
    target = viscosity[None]
    current = predicted
    for sweep_index in range(JACOBI):
        speed_pad = with_halo(current, (("down", 1), ("cross", 2)), 1)
        pulled = pair_pass(
            "jacobi",
            target,
            speed_pad * dens_pad[0:1],
            row_count,
            col_count,
            weights,
        )
        current = (predicted + TIME_STEP * (scale * inverse * pulled)) / diagonal
    moved_positions = positions + TIME_STEP * current
    field_six = jnp.concatenate([moved_positions, current], axis=0)
    keep_count = counts - moving
    result = place_arrivals(field_six, keep_count, moving)
    return (result[:3], result[3:])


def solution(mesh):
    return jax.shard_map(
        per_device,
        mesh=mesh,
        in_specs=(
            P(None, "down", "cross", None),
            P(None, "down", "cross", None),
            P("down", "cross", None),
            P("down", "cross", None),
            P("down", "cross"),
            P("down", "cross"),
        ),
        out_specs=(P(None, "down", "cross", None), P(None, "down", "cross", None)),
        check_vma=False,
    )
```

```python
import math

import jax
import jax.numpy as jnp
from jax import lax
from jax.experimental import pallas as pl
from jax.sharding import PartitionSpec as P

MOVE_MAX = 32
JACOBI = 2


KERNEL_NORM = 21.0 / (2.0 * math.pi)
PARTICLE_MASS = 0.02
REST_DENSITY = 1.0
STIFFNESS = 2.0
TIME_STEP = 0.05
GRAVITY_DOWN = 0.5
GRAVITY_UP = -1.0
NEIGHBOUR_STEPS = [(-1, -1), (-1, 0), (-1, 1), (0, -1), (0, 0), (0, 1), (1, -1), (1, 0), (1, 1)]


def with_halo(array, sides, width):
    for axis, dim in sides:
        count, length = (lax.axis_size(axis), array.shape[dim])
        up = [(i, (i + 1) % count) for i in range(count - 1)]
        down = [(j, i) for i, j in up]
        last = lax.slice_in_dim(array, length - width, length, axis=dim)
        initial = lax.slice_in_dim(array, 0, width, axis=dim)
        before = lax.ppermute(last, axis, up)
        after = lax.ppermute(initial, axis, down)
        array = jnp.concatenate([before, array, after], axis=dim)
    return array


def from_behind(block, axis, distance):
    devices = range(lax.axis_size(axis))
    route = [(i - distance, i) for i in devices if i - distance in devices]
    return lax.ppermute(block, axis, route)


def take_row(padded, lead_blocks, row_index, step_down, step_cross, col_count):
    whole_row = lax.dynamic_index_in_dim(
        padded, row_index + lead_blocks + step_down, axis=1, keepdims=False
    )
    return whole_row[:, lead_blocks + step_cross : lead_blocks + step_cross + col_count, :]


def separation(target, source, step_down, step_cross):
    offsets = (float(step_down), float(step_cross), 0.0)
    separations = [
        source[component][:, None, :] - target[component][:, :, None] + offsets[component]
        for component in range(3)
    ]
    distance = jnp.sqrt(
        separations[0] * separations[0]
        + separations[1] * separations[1]
        + separations[2] * separations[2]
    )
    falloff = jnp.maximum(1.0 - distance, 0.0)
    falloff_cubed = falloff * falloff * falloff
    weight = KERNEL_NORM * falloff_cubed * falloff * (4.0 * distance + 1.0)
    strength = 20.0 * KERNEL_NORM * falloff_cubed
    return (separations, weight, strength)


FAR_AWAY = 1.0e4
CHUNK = 128


def pair_pass(kind, target, source, row_count, col_count, weights=None):
    slot_count = target.shape[-1]
    block_count = row_count * col_count
    chunk_count = slot_count // CHUNK
    padded_cols = col_count + 2
    target_count = target.shape[0]
    source_count = source.shape[0]
    output_count = {"density": 2, "force": 4, "jacobi": 3}[kind]
    target_cols = jnp.moveaxis(target.reshape(target_count, block_count, slot_count), 0, 2)
    source_rows = source.reshape(source_count, (row_count + 2) * padded_cols, slot_count)

    def kernel(target_ref, source_ref, *refs):
        if kind == "force":
            out_ref, weight_ref = refs
        elif kind == "jacobi":
            weight_ref, out_ref = refs
        else:
            (out_ref,) = refs

        grid_block = None if kind == "jacobi" else pl.program_id(0)

        def body(step, carry):
            if kind == "jacobi":
                block = step // chunk_count
                first = pl.multiple_of((step % chunk_count) * CHUNK, CHUNK)
            else:
                block = grid_block
                first = pl.multiple_of(step * CHUNK, CHUNK)
            row = block // col_count
            col = block % col_count
            own = target_ref[block, pl.ds(first, CHUNK), :]
            mine = [
                jnp.broadcast_to(own[:, k : k + 1], (CHUNK, slot_count)) for k in range(target_count)
            ]
            totals = [jnp.zeros((CHUNK, slot_count), jnp.float32) for k in range(output_count)]
            for neighbour, (step_down, step_cross) in enumerate(NEIGHBOUR_STEPS):
                near = (row + 1 + step_down) * padded_cols + (col + 1 + step_cross)
                other = [source_ref[k, pl.ds(near, 1), :] for k in range(source_count)]
                if kind == "jacobi":
                    pull = weight_ref[step * 9 + neighbour]
                    for k in range(3):
                        totals[k] = totals[k] + pull * other[k]
                    continue
                gaps = [
                    other[0] + float(step_down) - mine[0],
                    other[1] + float(step_cross) - mine[1],
                    other[2] - mine[2],
                ]
                squared = gaps[0] * gaps[0] + gaps[1] * gaps[1] + gaps[2] * gaps[2]
                distance = squared * lax.rsqrt(jnp.maximum(squared, 1.0e-30))
                falloff = jnp.maximum(1.0 - distance, 0.0)
                cubed = falloff * falloff * falloff
                if kind == "density":
                    totals[0] = totals[0] + cubed * falloff * (4.0 * distance + 1.0)
                    spread = None
                    for k in range(3):
                        change = other[3 + k] - mine[3 + k]
                        term = change * change
                        spread = term if spread is None else spread + term
                    totals[1] = totals[1] + cubed * spread
                elif kind == "force":
                    push = (mine[3] + other[3]) * cubed
                    for k in range(3):
                        totals[k] = totals[k] + push * gaps[k]
                    pull = (mine[4] + other[5]) * cubed
                    weight_ref[step * 9 + neighbour] = pull
                    totals[3] = totals[3] + pull * other[4]
            lanes = lax.broadcasted_iota(jnp.int32, (CHUNK, slot_count), 1)
            table = jnp.zeros((CHUNK, slot_count), jnp.float32)
            for k in range(output_count):
                table = jnp.where(lanes == k, jnp.sum(totals[k], axis=1, keepdims=True), table)
            flipped = table.T
            for k in range(output_count):
                out_ref[k, pl.ds(block, 1), pl.ds(first, CHUNK)] = flipped[k : k + 1, :]
            return carry

        lax.fori_loop(0, block_count * chunk_count if kind == "jacobi" else chunk_count, body, 0)

    out_shape = jax.ShapeDtypeStruct((output_count, block_count, slot_count), jnp.float32)
    whole = [
        pl.BlockSpec(target_cols.shape, lambda block: (0, 0, 0)),
        pl.BlockSpec(source_rows.shape, lambda block: (0, 0, 0)),
    ]
    out_spec = pl.BlockSpec(out_shape.shape, lambda block: (0, 0, 0))
    weight_spec = pl.BlockSpec((chunk_count * 9, CHUNK, slot_count), lambda block: (block, 0, 0))
    grid = (block_count,)
    if kind == "force":
        weight_shape = jax.ShapeDtypeStruct(
            (block_count * chunk_count * 9, CHUNK, slot_count), jnp.float32
        )
        result, weights = pl.pallas_call(
            kernel,
            out_shape=(out_shape, weight_shape),
            grid=grid,
            in_specs=whole,
            out_specs=(out_spec, weight_spec),
        )(target_cols, source_rows)
    elif kind == "jacobi":
        result = pl.pallas_call(kernel, out_shape=out_shape)(target_cols, source_rows, weights)
    else:
        result = pl.pallas_call(
            kernel, out_shape=out_shape, grid=grid, in_specs=whole, out_specs=out_spec
        )(target_cols, source_rows)
    result = result.reshape(output_count, row_count, col_count, slot_count)
    if kind == "force":
        return result, weights
    return result


def shift_lanes(field, distance):
    slot_count = field.shape[-1]
    step = 1
    while step < slot_count:
        rolled = jnp.roll(field, -step, axis=-1)
        chosen = ((distance & step) != 0)[None, :, :, None]
        field = jnp.where(chosen, rolled, field)
        step *= 2
    return field


def place_arrivals(field_six, keep_count, moving):
    slot_count = field_six.shape[3]
    keep_plane = jnp.broadcast_to(keep_count[-1].astype(jnp.float32)[:, None], field_six.shape[2:])
    move_plane = jnp.broadcast_to(moving[-1].astype(jnp.float32)[:, None], field_six.shape[2:])
    edge_pack = jnp.concatenate([field_six[:, -1], keep_plane[None], move_plane[None]], axis=0)
    received = from_behind(edge_pack, "down", 1)
    source_field = jnp.concatenate([received[:6][:, None], field_six[:, :-1]], axis=1)
    source_keep = jnp.concatenate([received[6, :, 0].astype(jnp.int32)[None], keep_count[:-1]], axis=0)
    arriving = jnp.concatenate([received[7, :, 0].astype(jnp.int32)[None], moving[:-1]], axis=0)
    distance = jnp.mod(source_keep - keep_count, slot_count)
    incoming = shift_lanes(source_field, distance)
    incoming = jnp.concatenate([incoming[:1] - 1.0, incoming[1:]], axis=0)
    slot_ids = lax.broadcasted_iota(jnp.int32, field_six.shape[1:], 2)
    own_mask = slot_ids < keep_count[..., None]
    new_mask = (slot_ids >= keep_count[..., None]) & (
        slot_ids < (keep_count + arriving)[..., None]
    )
    return jnp.where(own_mask[None], field_six, jnp.where(new_mask[None], incoming, 0.0))


def per_device(positions, velocities, plastic_viscosity, yield_stress, counts, moving):
    row_count, col_count, slot_count = positions.shape[1:]
    slot_ids = lax.broadcasted_iota(jnp.int32, (row_count, col_count, slot_count), 2)
    live = (slot_ids < counts[:, :, None]).astype(jnp.float32)
    state = jnp.concatenate([positions, velocities, live[None]], axis=0)
    state_pad = with_halo(state, (("down", 1), ("cross", 2)), 1)
    far = jnp.where(state_pad[6:7] > 0.0, state_pad[:3], FAR_AWAY)
    sums = pair_pass(
        "density",
        jnp.concatenate([positions, velocities], axis=0),
        jnp.concatenate([far, state_pad[3:6]], axis=0),
        row_count,
        col_count,
    )
    density = PARTICLE_MASS * (KERNEL_NORM * sums[0] + KERNEL_NORM * (1.0 - live))
    strain = (PARTICLE_MASS * 20.0 * KERNEL_NORM) * sums[1]
    inverse = 1.0 / density
    pressure = STIFFNESS * (density - REST_DENSITY) * inverse * inverse
    viscosity = plastic_viscosity + yield_stress / jnp.sqrt(1.0 + strain)
    dens_pad = with_halo(jnp.stack([inverse, pressure, viscosity]), (("down", 1), ("cross", 2)), 1)
    forces, weights = pair_pass(
        "force",
        jnp.concatenate([positions, pressure[None], viscosity[None]], axis=0),
        jnp.concatenate([far, dens_pad[1:2], dens_pad[0:1], dens_pad[2:3]], axis=0),
        row_count,
        col_count,
    )
    scale = PARTICLE_MASS * 20.0 * KERNEL_NORM
    gravity = jnp.array([GRAVITY_DOWN, 0.0, GRAVITY_UP], jnp.float32)[:, None, None, None]
    predicted = velocities + TIME_STEP * (-scale * forces[:3] + gravity)
    diagonal = 1.0 + TIME_STEP * (scale * inverse * forces[3])
    target = viscosity[None]
    current = predicted
    for sweep_index in range(JACOBI):
        speed_pad = with_halo(current, (("down", 1), ("cross", 2)), 1)
        pulled = pair_pass(
            "jacobi",
            target,
            speed_pad * dens_pad[0:1],
            row_count,
            col_count,
            weights,
        )
        current = (predicted + TIME_STEP * (scale * inverse * pulled)) / diagonal
    moved_positions = positions + TIME_STEP * current
    field_six = jnp.concatenate([moved_positions, current], axis=0)
    keep_count = counts - moving
    result = place_arrivals(field_six, keep_count, moving)
    return (result[:3], result[3:])


def solution(mesh):
    return jax.shard_map(
        per_device,
        mesh=mesh,
        in_specs=(
            P(None, "down", "cross", None),
            P(None, "down", "cross", None),
            P("down", "cross", None),
            P("down", "cross", None),
            P("down", "cross"),
            P("down", "cross"),
        ),
        out_specs=(P(None, "down", "cross", None), P(None, "down", "cross", None)),
        check_vma=False,
    )
```

```python
import math

import jax
import jax.numpy as jnp
from jax import lax
from jax.experimental import pallas as pl
from jax.sharding import PartitionSpec as P

MOVE_MAX = 32
JACOBI = 2


KERNEL_NORM = 21.0 / (2.0 * math.pi)
PARTICLE_MASS = 0.02
REST_DENSITY = 1.0
STIFFNESS = 2.0
TIME_STEP = 0.05
GRAVITY_DOWN = 0.5
GRAVITY_UP = -1.0
NEIGHBOUR_STEPS = [(-1, -1), (-1, 0), (-1, 1), (0, -1), (0, 0), (0, 1), (1, -1), (1, 0), (1, 1)]


def with_halo(array, sides, width):
    for axis, dim in sides:
        count, length = (lax.axis_size(axis), array.shape[dim])
        up = [(i, (i + 1) % count) for i in range(count - 1)]
        down = [(j, i) for i, j in up]
        last = lax.slice_in_dim(array, length - width, length, axis=dim)
        initial = lax.slice_in_dim(array, 0, width, axis=dim)
        before = lax.ppermute(last, axis, up)
        after = lax.ppermute(initial, axis, down)
        array = jnp.concatenate([before, array, after], axis=dim)
    return array


def from_behind(block, axis, distance):
    devices = range(lax.axis_size(axis))
    route = [(i - distance, i) for i in devices if i - distance in devices]
    return lax.ppermute(block, axis, route)


def take_row(padded, lead_blocks, row_index, step_down, step_cross, col_count):
    whole_row = lax.dynamic_index_in_dim(
        padded, row_index + lead_blocks + step_down, axis=1, keepdims=False
    )
    return whole_row[:, lead_blocks + step_cross : lead_blocks + step_cross + col_count, :]


def separation(target, source, step_down, step_cross):
    offsets = (float(step_down), float(step_cross), 0.0)
    separations = [
        source[component][:, None, :] - target[component][:, :, None] + offsets[component]
        for component in range(3)
    ]
    distance = jnp.sqrt(
        separations[0] * separations[0]
        + separations[1] * separations[1]
        + separations[2] * separations[2]
    )
    falloff = jnp.maximum(1.0 - distance, 0.0)
    falloff_cubed = falloff * falloff * falloff
    weight = KERNEL_NORM * falloff_cubed * falloff * (4.0 * distance + 1.0)
    strength = 20.0 * KERNEL_NORM * falloff_cubed
    return (separations, weight, strength)


FAR_AWAY = 1.0e4
CHUNK = 128


def pair_pass(kind, target, source, row_count, col_count, weights=None):
    slot_count = target.shape[-1]
    block_count = row_count * col_count
    chunk_count = slot_count // CHUNK
    padded_cols = col_count + 2
    target_count = target.shape[0]
    source_count = source.shape[0]
    output_count = {"density": 2, "force": 4, "jacobi": 3}[kind]
    target_cols = target.reshape(target_count, block_count, slot_count)
    source_rows = source.reshape(source_count, (row_count + 2) * padded_cols, slot_count)

    def kernel(target_ref, source_ref, *refs):
        if kind == "force":
            out_ref, weight_ref = refs
        elif kind == "jacobi":
            weight_ref, out_ref = refs
        else:
            (out_ref,) = refs

        grid_block = None if kind == "jacobi" else pl.program_id(0)

        def body(step, carry):
            if kind == "jacobi":
                block = step // chunk_count
                first = pl.multiple_of((step % chunk_count) * CHUNK, CHUNK)
            else:
                block = grid_block
                first = pl.multiple_of(step * CHUNK, CHUNK)
            row = block // col_count
            col = block % col_count
            stacked = jnp.zeros((slot_count, slot_count), jnp.float32)
            planes = lax.broadcasted_iota(jnp.int32, (slot_count, slot_count), 0)
            for k in range(target_count):
                stacked = jnp.where(planes == k, target_ref[k, pl.ds(block, 1), :], stacked)
            own = stacked.T
            mine = [
                jnp.broadcast_to(own[:, k : k + 1], (CHUNK, slot_count)) for k in range(target_count)
            ]
            totals = [jnp.zeros((CHUNK, slot_count), jnp.float32) for k in range(output_count)]
            for neighbour, (step_down, step_cross) in enumerate(NEIGHBOUR_STEPS):
                near = (row + 1 + step_down) * padded_cols + (col + 1 + step_cross)
                other = [source_ref[k, pl.ds(near, 1), :] for k in range(source_count)]
                if kind == "jacobi":
                    pull = weight_ref[step * 9 + neighbour]
                    for k in range(3):
                        totals[k] = totals[k] + pull * other[k]
                    continue
                gaps = [
                    other[0] + float(step_down) - mine[0],
                    other[1] + float(step_cross) - mine[1],
                    other[2] - mine[2],
                ]
                squared = gaps[0] * gaps[0] + gaps[1] * gaps[1] + gaps[2] * gaps[2]
                distance = squared * lax.rsqrt(jnp.maximum(squared, 1.0e-30))
                falloff = jnp.maximum(1.0 - distance, 0.0)
                cubed = falloff * falloff * falloff
                if kind == "density":
                    totals[0] = totals[0] + cubed * falloff * (4.0 * distance + 1.0)
                    spread = None
                    for k in range(3):
                        change = other[3 + k] - mine[3 + k]
                        term = change * change
                        spread = term if spread is None else spread + term
                    totals[1] = totals[1] + cubed * spread
                elif kind == "force":
                    push = (mine[3] + other[3]) * cubed
                    for k in range(3):
                        totals[k] = totals[k] + push * gaps[k]
                    pull = (mine[4] + other[5]) * cubed
                    weight_ref[step * 9 + neighbour] = pull
                    totals[3] = totals[3] + pull * other[4]
            lanes = lax.broadcasted_iota(jnp.int32, (CHUNK, slot_count), 1)
            table = jnp.zeros((CHUNK, slot_count), jnp.float32)
            for k in range(output_count):
                table = jnp.where(lanes == k, jnp.sum(totals[k], axis=1, keepdims=True), table)
            flipped = table.T
            for k in range(output_count):
                out_ref[k, pl.ds(block, 1), pl.ds(first, CHUNK)] = flipped[k : k + 1, :]
            return carry

        lax.fori_loop(0, block_count * chunk_count if kind == "jacobi" else chunk_count, body, 0)

    out_shape = jax.ShapeDtypeStruct((output_count, block_count, slot_count), jnp.float32)
    whole = [
        pl.BlockSpec(target_cols.shape, lambda block: (0, 0, 0)),
        pl.BlockSpec(source_rows.shape, lambda block: (0, 0, 0)),
    ]
    out_spec = pl.BlockSpec(out_shape.shape, lambda block: (0, 0, 0))
    weight_spec = pl.BlockSpec((chunk_count * 9, CHUNK, slot_count), lambda block: (block, 0, 0))
    grid = (block_count,)
    if kind == "force":
        weight_shape = jax.ShapeDtypeStruct(
            (block_count * chunk_count * 9, CHUNK, slot_count), jnp.float32
        )
        result, weights = pl.pallas_call(
            kernel,
            out_shape=(out_shape, weight_shape),
            grid=grid,
            in_specs=whole,
            out_specs=(out_spec, weight_spec),
        )(target_cols, source_rows)
    elif kind == "jacobi":
        result = pl.pallas_call(kernel, out_shape=out_shape)(target_cols, source_rows, weights)
    else:
        result = pl.pallas_call(
            kernel, out_shape=out_shape, grid=grid, in_specs=whole, out_specs=out_spec
        )(target_cols, source_rows)
    result = result.reshape(output_count, row_count, col_count, slot_count)
    if kind == "force":
        return result, weights
    return result


def shift_lanes(field, distance):
    slot_count = field.shape[-1]
    step = 1
    while step < slot_count:
        rolled = jnp.roll(field, -step, axis=-1)
        chosen = ((distance & step) != 0)[None, :, :, None]
        field = jnp.where(chosen, rolled, field)
        step *= 2
    return field


def place_arrivals(field_six, keep_count, moving):
    slot_count = field_six.shape[3]
    keep_plane = jnp.broadcast_to(keep_count[-1].astype(jnp.float32)[:, None], field_six.shape[2:])
    move_plane = jnp.broadcast_to(moving[-1].astype(jnp.float32)[:, None], field_six.shape[2:])
    edge_pack = jnp.concatenate([field_six[:, -1], keep_plane[None], move_plane[None]], axis=0)
    received = from_behind(edge_pack, "down", 1)
    source_field = jnp.concatenate([received[:6][:, None], field_six[:, :-1]], axis=1)
    source_keep = jnp.concatenate([received[6, :, 0].astype(jnp.int32)[None], keep_count[:-1]], axis=0)
    arriving = jnp.concatenate([received[7, :, 0].astype(jnp.int32)[None], moving[:-1]], axis=0)
    distance = jnp.mod(source_keep - keep_count, slot_count)
    incoming = shift_lanes(source_field, distance)
    incoming = jnp.concatenate([incoming[:1] - 1.0, incoming[1:]], axis=0)
    slot_ids = lax.broadcasted_iota(jnp.int32, field_six.shape[1:], 2)
    own_mask = slot_ids < keep_count[..., None]
    new_mask = (slot_ids >= keep_count[..., None]) & (
        slot_ids < (keep_count + arriving)[..., None]
    )
    return jnp.where(own_mask[None], field_six, jnp.where(new_mask[None], incoming, 0.0))


def per_device(positions, velocities, plastic_viscosity, yield_stress, counts, moving):
    row_count, col_count, slot_count = positions.shape[1:]
    slot_ids = lax.broadcasted_iota(jnp.int32, (row_count, col_count, slot_count), 2)
    live = (slot_ids < counts[:, :, None]).astype(jnp.float32)
    state = jnp.concatenate([positions, velocities, live[None]], axis=0)
    state_pad = with_halo(state, (("down", 1), ("cross", 2)), 1)
    far = jnp.where(state_pad[6:7] > 0.0, state_pad[:3], FAR_AWAY)
    sums = pair_pass(
        "density",
        jnp.concatenate([positions, velocities], axis=0),
        jnp.concatenate([far, state_pad[3:6]], axis=0),
        row_count,
        col_count,
    )
    density = PARTICLE_MASS * (KERNEL_NORM * sums[0] + KERNEL_NORM * (1.0 - live))
    strain = (PARTICLE_MASS * 20.0 * KERNEL_NORM) * sums[1]
    inverse = 1.0 / density
    pressure = STIFFNESS * (density - REST_DENSITY) * inverse * inverse
    viscosity = plastic_viscosity + yield_stress / jnp.sqrt(1.0 + strain)
    dens_pad = with_halo(jnp.stack([inverse, pressure, viscosity]), (("down", 1), ("cross", 2)), 1)
    forces, weights = pair_pass(
        "force",
        jnp.concatenate([positions, pressure[None], viscosity[None]], axis=0),
        jnp.concatenate([far, dens_pad[1:2], dens_pad[0:1], dens_pad[2:3]], axis=0),
        row_count,
        col_count,
    )
    scale = PARTICLE_MASS * 20.0 * KERNEL_NORM
    gravity = jnp.array([GRAVITY_DOWN, 0.0, GRAVITY_UP], jnp.float32)[:, None, None, None]
    predicted = velocities + TIME_STEP * (-scale * forces[:3] + gravity)
    diagonal = 1.0 + TIME_STEP * (scale * inverse * forces[3])
    target = viscosity[None]
    current = predicted
    for sweep_index in range(JACOBI):
        speed_pad = with_halo(current, (("down", 1), ("cross", 2)), 1)
        pulled = pair_pass(
            "jacobi",
            target,
            speed_pad * dens_pad[0:1],
            row_count,
            col_count,
            weights,
        )
        current = (predicted + TIME_STEP * (scale * inverse * pulled)) / diagonal
    moved_positions = positions + TIME_STEP * current
    field_six = jnp.concatenate([moved_positions, current], axis=0)
    keep_count = counts - moving
    result = place_arrivals(field_six, keep_count, moving)
    return (result[:3], result[3:])


def solution(mesh):
    return jax.shard_map(
        per_device,
        mesh=mesh,
        in_specs=(
            P(None, "down", "cross", None),
            P(None, "down", "cross", None),
            P("down", "cross", None),
            P("down", "cross", None),
            P("down", "cross"),
            P("down", "cross"),
        ),
        out_specs=(P(None, "down", "cross", None), P(None, "down", "cross", None)),
        check_vma=False,
    )
```

```python
import math

import jax
import jax.numpy as jnp
from jax import lax
from jax.experimental import pallas as pl
from jax.sharding import PartitionSpec as P

MOVE_MAX = 32
JACOBI = 2


KERNEL_NORM = 21.0 / (2.0 * math.pi)
PARTICLE_MASS = 0.02
REST_DENSITY = 1.0
STIFFNESS = 2.0
TIME_STEP = 0.05
GRAVITY_DOWN = 0.5
GRAVITY_UP = -1.0
NEIGHBOUR_STEPS = [(-1, -1), (-1, 0), (-1, 1), (0, -1), (0, 0), (0, 1), (1, -1), (1, 0), (1, 1)]


def with_halo(array, sides, width):
    for axis, dim in sides:
        count, length = (lax.axis_size(axis), array.shape[dim])
        up = [(i, (i + 1) % count) for i in range(count - 1)]
        down = [(j, i) for i, j in up]
        last = lax.slice_in_dim(array, length - width, length, axis=dim)
        initial = lax.slice_in_dim(array, 0, width, axis=dim)
        before = lax.ppermute(last, axis, up)
        after = lax.ppermute(initial, axis, down)
        array = jnp.concatenate([before, array, after], axis=dim)
    return array


def from_behind(block, axis, distance):
    devices = range(lax.axis_size(axis))
    route = [(i - distance, i) for i in devices if i - distance in devices]
    return lax.ppermute(block, axis, route)


def take_row(padded, lead_blocks, row_index, step_down, step_cross, col_count):
    whole_row = lax.dynamic_index_in_dim(
        padded, row_index + lead_blocks + step_down, axis=1, keepdims=False
    )
    return whole_row[:, lead_blocks + step_cross : lead_blocks + step_cross + col_count, :]


def separation(target, source, step_down, step_cross):
    offsets = (float(step_down), float(step_cross), 0.0)
    separations = [
        source[component][:, None, :] - target[component][:, :, None] + offsets[component]
        for component in range(3)
    ]
    distance = jnp.sqrt(
        separations[0] * separations[0]
        + separations[1] * separations[1]
        + separations[2] * separations[2]
    )
    falloff = jnp.maximum(1.0 - distance, 0.0)
    falloff_cubed = falloff * falloff * falloff
    weight = KERNEL_NORM * falloff_cubed * falloff * (4.0 * distance + 1.0)
    strength = 20.0 * KERNEL_NORM * falloff_cubed
    return (separations, weight, strength)


FAR_AWAY = 1.0e4
CHUNK = 128


def pair_pass(kind, target, source, row_count, col_count, weights=None):
    slot_count = target.shape[-1]
    block_count = row_count * col_count
    chunk_count = slot_count // CHUNK
    padded_cols = col_count + 2
    target_count = target.shape[0]
    source_count = source.shape[0]
    output_count = {"density": 2, "force": 4, "jacobi": 3}[kind]
    target_cols = target.reshape(target_count, block_count, slot_count)
    source_rows = source.reshape(source_count, (row_count + 2) * padded_cols, slot_count)

    def kernel(target_ref, source_ref, *refs):
        if kind == "force":
            out_ref, weight_ref = refs
        elif kind == "jacobi":
            weight_ref, out_ref = refs
        else:
            (out_ref,) = refs

        block = pl.program_id(0)

        def body(step, carry):
            first = pl.multiple_of(step * CHUNK, CHUNK)
            row = block // col_count
            col = block % col_count
            stacked = jnp.zeros((slot_count, slot_count), jnp.float32)
            planes = lax.broadcasted_iota(jnp.int32, (slot_count, slot_count), 0)
            for k in range(target_count):
                stacked = jnp.where(planes == k, target_ref[k, pl.ds(block, 1), :], stacked)
            own = stacked.T
            mine = [
                jnp.broadcast_to(own[:, k : k + 1], (CHUNK, slot_count)) for k in range(target_count)
            ]
            totals = [jnp.zeros((CHUNK, slot_count), jnp.float32) for k in range(output_count)]
            for neighbour, (step_down, step_cross) in enumerate(NEIGHBOUR_STEPS):
                near = (row + 1 + step_down) * padded_cols + (col + 1 + step_cross)
                other = [source_ref[k, pl.ds(near, 1), :] for k in range(source_count)]
                if kind == "jacobi":
                    pull = weight_ref[step * 9 + neighbour]
                    for k in range(3):
                        totals[k] = totals[k] + pull * other[k]
                    continue
                gaps = [
                    other[0] + float(step_down) - mine[0],
                    other[1] + float(step_cross) - mine[1],
                    other[2] - mine[2],
                ]
                squared = gaps[0] * gaps[0] + gaps[1] * gaps[1] + gaps[2] * gaps[2]
                distance = squared * lax.rsqrt(jnp.maximum(squared, 1.0e-30))
                falloff = jnp.maximum(1.0 - distance, 0.0)
                cubed = falloff * falloff * falloff
                if kind == "density":
                    totals[0] = totals[0] + cubed * falloff * (4.0 * distance + 1.0)
                    spread = None
                    for k in range(3):
                        change = other[3 + k] - mine[3 + k]
                        term = change * change
                        spread = term if spread is None else spread + term
                    totals[1] = totals[1] + cubed * spread
                elif kind == "force":
                    push = (mine[3] + other[3]) * cubed
                    for k in range(3):
                        totals[k] = totals[k] + push * gaps[k]
                    pull = (mine[4] + other[5]) * cubed
                    weight_ref[step * 9 + neighbour] = pull
                    totals[3] = totals[3] + pull * other[4]
            lanes = lax.broadcasted_iota(jnp.int32, (CHUNK, slot_count), 1)
            table = jnp.zeros((CHUNK, slot_count), jnp.float32)
            for k in range(output_count):
                table = jnp.where(lanes == k, jnp.sum(totals[k], axis=1, keepdims=True), table)
            flipped = table.T
            for k in range(output_count):
                out_ref[k, pl.ds(block, 1), pl.ds(first, CHUNK)] = flipped[k : k + 1, :]
            return carry

        lax.fori_loop(0, chunk_count, body, 0)

    out_shape = jax.ShapeDtypeStruct((output_count, block_count, slot_count), jnp.float32)
    whole = [
        pl.BlockSpec(target_cols.shape, lambda block: (0, 0, 0)),
        pl.BlockSpec(source_rows.shape, lambda block: (0, 0, 0)),
    ]
    out_spec = pl.BlockSpec(out_shape.shape, lambda block: (0, 0, 0))
    weight_spec = pl.BlockSpec((chunk_count * 9, CHUNK, slot_count), lambda block: (block, 0, 0))
    grid = (block_count,)
    if kind == "force":
        weight_shape = jax.ShapeDtypeStruct(
            (block_count * chunk_count * 9, CHUNK, slot_count), jnp.float32
        )
        result, weights = pl.pallas_call(
            kernel,
            out_shape=(out_shape, weight_shape),
            grid=grid,
            in_specs=whole,
            out_specs=(out_spec, weight_spec),
        )(target_cols, source_rows)
    elif kind == "jacobi":
        result = pl.pallas_call(
            kernel,
            out_shape=out_shape,
            grid=grid,
            in_specs=whole + [weight_spec],
            out_specs=out_spec,
        )(target_cols, source_rows, weights)
    else:
        result = pl.pallas_call(
            kernel, out_shape=out_shape, grid=grid, in_specs=whole, out_specs=out_spec
        )(target_cols, source_rows)
    result = result.reshape(output_count, row_count, col_count, slot_count)
    if kind == "force":
        return result, weights
    return result


def shift_lanes(field, distance):
    slot_count = field.shape[-1]
    step = 1
    while step < slot_count:
        rolled = jnp.roll(field, -step, axis=-1)
        chosen = ((distance & step) != 0)[None, :, :, None]
        field = jnp.where(chosen, rolled, field)
        step *= 2
    return field


def place_arrivals(field_six, keep_count, moving):
    slot_count = field_six.shape[3]
    keep_plane = jnp.broadcast_to(keep_count[-1].astype(jnp.float32)[:, None], field_six.shape[2:])
    move_plane = jnp.broadcast_to(moving[-1].astype(jnp.float32)[:, None], field_six.shape[2:])
    edge_pack = jnp.concatenate([field_six[:, -1], keep_plane[None], move_plane[None]], axis=0)
    received = from_behind(edge_pack, "down", 1)
    source_field = jnp.concatenate([received[:6][:, None], field_six[:, :-1]], axis=1)
    source_keep = jnp.concatenate([received[6, :, 0].astype(jnp.int32)[None], keep_count[:-1]], axis=0)
    arriving = jnp.concatenate([received[7, :, 0].astype(jnp.int32)[None], moving[:-1]], axis=0)
    distance = jnp.mod(source_keep - keep_count, slot_count)
    incoming = shift_lanes(source_field, distance)
    incoming = jnp.concatenate([incoming[:1] - 1.0, incoming[1:]], axis=0)
    slot_ids = lax.broadcasted_iota(jnp.int32, field_six.shape[1:], 2)
    own_mask = slot_ids < keep_count[..., None]
    new_mask = (slot_ids >= keep_count[..., None]) & (
        slot_ids < (keep_count + arriving)[..., None]
    )
    return jnp.where(own_mask[None], field_six, jnp.where(new_mask[None], incoming, 0.0))


def per_device(positions, velocities, plastic_viscosity, yield_stress, counts, moving):
    row_count, col_count, slot_count = positions.shape[1:]
    slot_ids = lax.broadcasted_iota(jnp.int32, (row_count, col_count, slot_count), 2)
    live = (slot_ids < counts[:, :, None]).astype(jnp.float32)
    state = jnp.concatenate([positions, velocities, live[None]], axis=0)
    state_pad = with_halo(state, (("down", 1), ("cross", 2)), 1)
    far = jnp.where(state_pad[6:7] > 0.0, state_pad[:3], FAR_AWAY)
    sums = pair_pass(
        "density",
        jnp.concatenate([positions, velocities], axis=0),
        jnp.concatenate([far, state_pad[3:6]], axis=0),
        row_count,
        col_count,
    )
    density = PARTICLE_MASS * (KERNEL_NORM * sums[0] + KERNEL_NORM * (1.0 - live))
    strain = (PARTICLE_MASS * 20.0 * KERNEL_NORM) * sums[1]
    inverse = 1.0 / density
    pressure = STIFFNESS * (density - REST_DENSITY) * inverse * inverse
    viscosity = plastic_viscosity + yield_stress / jnp.sqrt(1.0 + strain)
    dens_pad = with_halo(jnp.stack([inverse, pressure, viscosity]), (("down", 1), ("cross", 2)), 1)
    forces, weights = pair_pass(
        "force",
        jnp.concatenate([positions, pressure[None], viscosity[None]], axis=0),
        jnp.concatenate([far, dens_pad[1:2], dens_pad[0:1], dens_pad[2:3]], axis=0),
        row_count,
        col_count,
    )
    scale = PARTICLE_MASS * 20.0 * KERNEL_NORM
    gravity = jnp.array([GRAVITY_DOWN, 0.0, GRAVITY_UP], jnp.float32)[:, None, None, None]
    predicted = velocities + TIME_STEP * (-scale * forces[:3] + gravity)
    diagonal = 1.0 + TIME_STEP * (scale * inverse * forces[3])
    target = viscosity[None]
    current = predicted
    for sweep_index in range(JACOBI):
        speed_pad = with_halo(current, (("down", 1), ("cross", 2)), 1)
        pulled = pair_pass(
            "jacobi",
            target,
            speed_pad * dens_pad[0:1],
            row_count,
            col_count,
            weights,
        )
        current = (predicted + TIME_STEP * (scale * inverse * pulled)) / diagonal
    moved_positions = positions + TIME_STEP * current
    field_six = jnp.concatenate([moved_positions, current], axis=0)
    keep_count = counts - moving
    result = place_arrivals(field_six, keep_count, moving)
    return (result[:3], result[3:])


def solution(mesh):
    return jax.shard_map(
        per_device,
        mesh=mesh,
        in_specs=(
            P(None, "down", "cross", None),
            P(None, "down", "cross", None),
            P("down", "cross", None),
            P("down", "cross", None),
            P("down", "cross"),
            P("down", "cross"),
        ),
        out_specs=(P(None, "down", "cross", None), P(None, "down", "cross", None)),
        check_vma=False,
    )
```

```python
import math

import jax
import jax.numpy as jnp
from jax import lax
from jax.experimental import pallas as pl
from jax.sharding import PartitionSpec as P

MOVE_MAX = 32
JACOBI = 2


KERNEL_NORM = 21.0 / (2.0 * math.pi)
PARTICLE_MASS = 0.02
REST_DENSITY = 1.0
STIFFNESS = 2.0
TIME_STEP = 0.05
GRAVITY_DOWN = 0.5
GRAVITY_UP = -1.0
NEIGHBOUR_STEPS = [(-1, -1), (-1, 0), (-1, 1), (0, -1), (0, 0), (0, 1), (1, -1), (1, 0), (1, 1)]


def with_halo(array, sides, width):
    for axis, dim in sides:
        count, length = (lax.axis_size(axis), array.shape[dim])
        up = [(i, (i + 1) % count) for i in range(count - 1)]
        down = [(j, i) for i, j in up]
        last = lax.slice_in_dim(array, length - width, length, axis=dim)
        initial = lax.slice_in_dim(array, 0, width, axis=dim)
        before = lax.ppermute(last, axis, up)
        after = lax.ppermute(initial, axis, down)
        array = jnp.concatenate([before, array, after], axis=dim)
    return array


def from_behind(block, axis, distance):
    devices = range(lax.axis_size(axis))
    route = [(i - distance, i) for i in devices if i - distance in devices]
    return lax.ppermute(block, axis, route)


def take_row(padded, lead_blocks, row_index, step_down, step_cross, col_count):
    whole_row = lax.dynamic_index_in_dim(
        padded, row_index + lead_blocks + step_down, axis=1, keepdims=False
    )
    return whole_row[:, lead_blocks + step_cross : lead_blocks + step_cross + col_count, :]


def separation(target, source, step_down, step_cross):
    offsets = (float(step_down), float(step_cross), 0.0)
    separations = [
        source[component][:, None, :] - target[component][:, :, None] + offsets[component]
        for component in range(3)
    ]
    distance = jnp.sqrt(
        separations[0] * separations[0]
        + separations[1] * separations[1]
        + separations[2] * separations[2]
    )
    falloff = jnp.maximum(1.0 - distance, 0.0)
    falloff_cubed = falloff * falloff * falloff
    weight = KERNEL_NORM * falloff_cubed * falloff * (4.0 * distance + 1.0)
    strength = 20.0 * KERNEL_NORM * falloff_cubed
    return (separations, weight, strength)


FAR_AWAY = 1.0e4
CHUNK = 128


def pair_pass(kind, target, source, row_count, col_count, weights=None):
    slot_count = target.shape[-1]
    block_count = row_count * col_count
    chunk_count = slot_count // CHUNK
    padded_cols = col_count + 2
    target_count = target.shape[0]
    source_count = source.shape[0]
    output_count = {"density": 2, "force": 3}.get(kind, source_count)
    target_cols = target.reshape(target_count, block_count, slot_count)
    source_rows = source.reshape(source_count, (row_count + 2) * padded_cols, slot_count)

    def kernel(target_ref, source_ref, *refs):
        if kind == "force":
            out_ref, weight_ref = refs
        elif kind == "jacobi":
            weight_ref, out_ref = refs
        else:
            (out_ref,) = refs

        grid_block = None if kind == "jacobi" else pl.program_id(0)

        def body(step, carry):
            if kind == "jacobi":
                block = step // chunk_count
                first = pl.multiple_of((step % chunk_count) * CHUNK, CHUNK)
            else:
                block = grid_block
                first = pl.multiple_of(step * CHUNK, CHUNK)
            row = block // col_count
            col = block % col_count
            stacked = jnp.zeros((slot_count, slot_count), jnp.float32)
            planes = lax.broadcasted_iota(jnp.int32, (slot_count, slot_count), 0)
            for k in range(target_count):
                stacked = jnp.where(planes == k, target_ref[k, pl.ds(block, 1), :], stacked)
            own = stacked.T
            mine = [
                jnp.broadcast_to(own[:, k : k + 1], (CHUNK, slot_count)) for k in range(target_count)
            ]
            totals = [jnp.zeros((CHUNK, slot_count), jnp.float32) for k in range(output_count)]
            for neighbour, (step_down, step_cross) in enumerate(NEIGHBOUR_STEPS):
                near = (row + 1 + step_down) * padded_cols + (col + 1 + step_cross)
                other = [source_ref[k, pl.ds(near, 1), :] for k in range(source_count)]
                if kind == "jacobi":
                    pull = weight_ref[step * 9 + neighbour]
                    for k in range(source_count):
                        totals[k] = totals[k] + pull * other[k]
                    continue
                gaps = [
                    other[0] + float(step_down) - mine[0],
                    other[1] + float(step_cross) - mine[1],
                    other[2] - mine[2],
                ]
                squared = gaps[0] * gaps[0] + gaps[1] * gaps[1] + gaps[2] * gaps[2]
                distance = squared * lax.rsqrt(jnp.maximum(squared, 1.0e-30))
                falloff = jnp.maximum(1.0 - distance, 0.0)
                cubed = falloff * falloff * falloff
                if kind == "density":
                    totals[0] = totals[0] + cubed * falloff * (4.0 * distance + 1.0)
                    spread = None
                    for k in range(3):
                        change = other[3 + k] - mine[3 + k]
                        term = change * change
                        spread = term if spread is None else spread + term
                    totals[1] = totals[1] + cubed * spread
                elif kind == "force":
                    push = (mine[3] + other[3]) * cubed
                    for k in range(3):
                        totals[k] = totals[k] + push * gaps[k]
                    pull = (mine[4] + other[5]) * cubed
                    weight_ref[step * 9 + neighbour] = pull
            lanes = lax.broadcasted_iota(jnp.int32, (CHUNK, slot_count), 1)
            table = jnp.zeros((CHUNK, slot_count), jnp.float32)
            for k in range(output_count):
                table = jnp.where(lanes == k, jnp.sum(totals[k], axis=1, keepdims=True), table)
            flipped = table.T
            for k in range(output_count):
                out_ref[k, pl.ds(block, 1), pl.ds(first, CHUNK)] = flipped[k : k + 1, :]
            return carry

        lax.fori_loop(0, block_count * chunk_count if kind == "jacobi" else chunk_count, body, 0)

    out_shape = jax.ShapeDtypeStruct((output_count, block_count, slot_count), jnp.float32)
    whole = [
        pl.BlockSpec(target_cols.shape, lambda block: (0, 0, 0)),
        pl.BlockSpec(source_rows.shape, lambda block: (0, 0, 0)),
    ]
    out_spec = pl.BlockSpec(out_shape.shape, lambda block: (0, 0, 0))
    weight_spec = pl.BlockSpec((chunk_count * 9, CHUNK, slot_count), lambda block: (block, 0, 0))
    grid = (block_count,)
    if kind == "force":
        weight_shape = jax.ShapeDtypeStruct(
            (block_count * chunk_count * 9, CHUNK, slot_count), jnp.float32
        )
        result, weights = pl.pallas_call(
            kernel,
            out_shape=(out_shape, weight_shape),
            grid=grid,
            in_specs=whole,
            out_specs=(out_spec, weight_spec),
        )(target_cols, source_rows)
    elif kind == "jacobi":
        result = pl.pallas_call(kernel, out_shape=out_shape)(target_cols, source_rows, weights)
    else:
        result = pl.pallas_call(
            kernel, out_shape=out_shape, grid=grid, in_specs=whole, out_specs=out_spec
        )(target_cols, source_rows)
    result = result.reshape(output_count, row_count, col_count, slot_count)
    if kind == "force":
        return result, weights
    return result


def shift_lanes(field, distance):
    slot_count = field.shape[-1]
    step = 1
    while step < slot_count:
        rolled = jnp.roll(field, -step, axis=-1)
        chosen = ((distance & step) != 0)[None, :, :, None]
        field = jnp.where(chosen, rolled, field)
        step *= 2
    return field


def place_arrivals(field_six, keep_count, moving):
    slot_count = field_six.shape[3]
    keep_plane = jnp.broadcast_to(keep_count[-1].astype(jnp.float32)[:, None], field_six.shape[2:])
    move_plane = jnp.broadcast_to(moving[-1].astype(jnp.float32)[:, None], field_six.shape[2:])
    edge_pack = jnp.concatenate([field_six[:, -1], keep_plane[None], move_plane[None]], axis=0)
    received = from_behind(edge_pack, "down", 1)
    source_field = jnp.concatenate([received[:6][:, None], field_six[:, :-1]], axis=1)
    source_keep = jnp.concatenate([received[6, :, 0].astype(jnp.int32)[None], keep_count[:-1]], axis=0)
    arriving = jnp.concatenate([received[7, :, 0].astype(jnp.int32)[None], moving[:-1]], axis=0)
    distance = jnp.mod(source_keep - keep_count, slot_count)
    incoming = shift_lanes(source_field, distance)
    incoming = jnp.concatenate([incoming[:1] - 1.0, incoming[1:]], axis=0)
    slot_ids = lax.broadcasted_iota(jnp.int32, field_six.shape[1:], 2)
    own_mask = slot_ids < keep_count[..., None]
    new_mask = (slot_ids >= keep_count[..., None]) & (
        slot_ids < (keep_count + arriving)[..., None]
    )
    return jnp.where(own_mask[None], field_six, jnp.where(new_mask[None], incoming, 0.0))


def per_device(positions, velocities, plastic_viscosity, yield_stress, counts, moving):
    row_count, col_count, slot_count = positions.shape[1:]
    slot_ids = lax.broadcasted_iota(jnp.int32, (row_count, col_count, slot_count), 2)
    live = (slot_ids < counts[:, :, None]).astype(jnp.float32)
    state = jnp.concatenate([positions, velocities, live[None]], axis=0)
    state_pad = with_halo(state, (("down", 1), ("cross", 2)), 1)
    far = jnp.where(state_pad[6:7] > 0.0, state_pad[:3], FAR_AWAY)
    sums = pair_pass(
        "density",
        jnp.concatenate([positions, velocities], axis=0),
        jnp.concatenate([far, state_pad[3:6]], axis=0),
        row_count,
        col_count,
    )
    density = PARTICLE_MASS * (KERNEL_NORM * sums[0] + KERNEL_NORM * (1.0 - live))
    strain = (PARTICLE_MASS * 20.0 * KERNEL_NORM) * sums[1]
    inverse = 1.0 / density
    pressure = STIFFNESS * (density - REST_DENSITY) * inverse * inverse
    viscosity = plastic_viscosity + yield_stress / jnp.sqrt(1.0 + strain)
    dens_pad = with_halo(jnp.stack([inverse, pressure, viscosity]), (("down", 1), ("cross", 2)), 1)
    forces, weights = pair_pass(
        "force",
        jnp.concatenate([positions, pressure[None], viscosity[None]], axis=0),
        jnp.concatenate([far, dens_pad[1:2], dens_pad[0:1], dens_pad[2:3]], axis=0),
        row_count,
        col_count,
    )
    scale = PARTICLE_MASS * 20.0 * KERNEL_NORM
    gravity = jnp.array([GRAVITY_DOWN, 0.0, GRAVITY_UP], jnp.float32)[:, None, None, None]
    predicted = velocities + TIME_STEP * (-scale * forces[:3] + gravity)
    target = viscosity[None]
    current = predicted
    diagonal = None
    for sweep_index in range(JACOBI):
        speed_pad = with_halo(current, (("down", 1), ("cross", 2)), 1)
        source = speed_pad * dens_pad[0:1]
        if diagonal is None:
            source = jnp.concatenate([source, dens_pad[0:1]], axis=0)
        pulled = pair_pass("jacobi", target, source, row_count, col_count, weights)
        if diagonal is None:
            diagonal = 1.0 + TIME_STEP * (scale * inverse * pulled[3])
            pulled = pulled[:3]
        current = (predicted + TIME_STEP * (scale * inverse * pulled)) / diagonal
    moved_positions = positions + TIME_STEP * current
    field_six = jnp.concatenate([moved_positions, current], axis=0)
    keep_count = counts - moving
    result = place_arrivals(field_six, keep_count, moving)
    return (result[:3], result[3:])


def solution(mesh):
    return jax.shard_map(
        per_device,
        mesh=mesh,
        in_specs=(
            P(None, "down", "cross", None),
            P(None, "down", "cross", None),
            P("down", "cross", None),
            P("down", "cross", None),
            P("down", "cross"),
            P("down", "cross"),
        ),
        out_specs=(P(None, "down", "cross", None), P(None, "down", "cross", None)),
        check_vma=False,
    )
```

```python
import math

import jax
import jax.numpy as jnp
from jax import lax
from jax.experimental import pallas as pl
from jax.sharding import PartitionSpec as P

MOVE_MAX = 32
JACOBI = 2


KERNEL_NORM = 21.0 / (2.0 * math.pi)
PARTICLE_MASS = 0.02
REST_DENSITY = 1.0
STIFFNESS = 2.0
TIME_STEP = 0.05
GRAVITY_DOWN = 0.5
GRAVITY_UP = -1.0
NEIGHBOUR_STEPS = [(-1, -1), (-1, 0), (-1, 1), (0, -1), (0, 0), (0, 1), (1, -1), (1, 0), (1, 1)]


def with_halo(array, sides, width):
    for axis, dim in sides:
        count, length = (lax.axis_size(axis), array.shape[dim])
        up = [(i, (i + 1) % count) for i in range(count - 1)]
        down = [(j, i) for i, j in up]
        last = lax.slice_in_dim(array, length - width, length, axis=dim)
        initial = lax.slice_in_dim(array, 0, width, axis=dim)
        before = lax.ppermute(last, axis, up)
        after = lax.ppermute(initial, axis, down)
        array = jnp.concatenate([before, array, after], axis=dim)
    return array


def from_behind(block, axis, distance):
    devices = range(lax.axis_size(axis))
    route = [(i - distance, i) for i in devices if i - distance in devices]
    return lax.ppermute(block, axis, route)


def take_row(padded, lead_blocks, row_index, step_down, step_cross, col_count):
    whole_row = lax.dynamic_index_in_dim(
        padded, row_index + lead_blocks + step_down, axis=1, keepdims=False
    )
    return whole_row[:, lead_blocks + step_cross : lead_blocks + step_cross + col_count, :]


def separation(target, source, step_down, step_cross):
    offsets = (float(step_down), float(step_cross), 0.0)
    separations = [
        source[component][:, None, :] - target[component][:, :, None] + offsets[component]
        for component in range(3)
    ]
    distance = jnp.sqrt(
        separations[0] * separations[0]
        + separations[1] * separations[1]
        + separations[2] * separations[2]
    )
    falloff = jnp.maximum(1.0 - distance, 0.0)
    falloff_cubed = falloff * falloff * falloff
    weight = KERNEL_NORM * falloff_cubed * falloff * (4.0 * distance + 1.0)
    strength = 20.0 * KERNEL_NORM * falloff_cubed
    return (separations, weight, strength)


FAR_AWAY = 1.0e4
CHUNK = 128


def pair_pass(kind, target, source, row_count, col_count, weights=None):
    slot_count = target.shape[-1]
    block_count = row_count * col_count
    chunk_count = slot_count // CHUNK
    padded_cols = col_count + 2
    target_count = target.shape[0]
    source_count = source.shape[0]
    output_count = {"density": 2, "force": 4, "jacobi": 3}[kind]
    target_cols = target.reshape(target_count, block_count, slot_count)
    source_rows = source.reshape(source_count, (row_count + 2) * padded_cols, slot_count)

    def kernel(target_ref, source_ref, *refs):
        if kind == "force":
            out_ref, weight_ref = refs
        elif kind == "jacobi":
            weight_ref, out_ref = refs
        else:
            (out_ref,) = refs

        grid_block = None if kind == "jacobi" else pl.program_id(0)

        def body(step, carry):
            if kind == "jacobi":
                block = step // chunk_count
                first = pl.multiple_of((step % chunk_count) * CHUNK, CHUNK)
            else:
                block = grid_block
                first = pl.multiple_of(step * CHUNK, CHUNK)
            row = block // col_count
            col = block % col_count
            stacked = jnp.zeros((slot_count, slot_count), jnp.float32)
            planes = lax.broadcasted_iota(jnp.int32, (slot_count, slot_count), 0)
            for k in range(target_count):
                stacked = jnp.where(planes == k, target_ref[k, pl.ds(block, 1), :], stacked)
            own = stacked.T
            mine = [
                jnp.broadcast_to(own[:, k : k + 1], (CHUNK, slot_count)) for k in range(target_count)
            ]
            totals = [jnp.zeros((CHUNK, slot_count), jnp.float32) for k in range(output_count)]
            for neighbour, (step_down, step_cross) in enumerate(NEIGHBOUR_STEPS):
                near = (row + 1 + step_down) * padded_cols + (col + 1 + step_cross)
                other = [source_ref[k, pl.ds(near, 1), :] for k in range(source_count)]
                if kind == "jacobi":
                    pull = weight_ref[step * 9 + neighbour]
                    for k in range(3):
                        totals[k] = totals[k] + pull * other[k]
                    continue
                gaps = [
                    other[0] + float(step_down) - mine[0],
                    other[1] + float(step_cross) - mine[1],
                    other[2] - mine[2],
                ]
                squared = gaps[0] * gaps[0] + gaps[1] * gaps[1] + gaps[2] * gaps[2]
                distance = squared * lax.rsqrt(jnp.maximum(squared, 1.0e-30))
                falloff = jnp.maximum(1.0 - distance, 0.0)
                cubed = falloff * falloff * falloff
                if kind == "density":
                    totals[0] = totals[0] + cubed * falloff * (4.0 * distance + 1.0)
                    spread = None
                    for k in range(3):
                        change = other[3 + k] - mine[3 + k]
                        term = change * change
                        spread = term if spread is None else spread + term
                    totals[1] = totals[1] + cubed * spread
                elif kind == "force":
                    push = (mine[3] + other[3]) * cubed
                    for k in range(3):
                        totals[k] = totals[k] + push * gaps[k]
                    pull = (mine[4] + other[5]) * cubed
                    weight_ref[step * 9 + neighbour] = pull
                    totals[3] = totals[3] + pull * other[4]
            lanes = lax.broadcasted_iota(jnp.int32, (CHUNK, slot_count), 1)
            table = jnp.zeros((CHUNK, slot_count), jnp.float32)
            for k in range(output_count):
                table = jnp.where(lanes == k, jnp.sum(totals[k], axis=1, keepdims=True), table)
            flipped = table.T
            for k in range(output_count):
                out_ref[k, pl.ds(block, 1), pl.ds(first, CHUNK)] = flipped[k : k + 1, :]
            return carry

        lax.fori_loop(
            0, block_count * chunk_count if kind == "jacobi" else chunk_count, body, 0, unroll=True
        )

    out_shape = jax.ShapeDtypeStruct((output_count, block_count, slot_count), jnp.float32)
    whole = [
        pl.BlockSpec(target_cols.shape, lambda block: (0, 0, 0)),
        pl.BlockSpec(source_rows.shape, lambda block: (0, 0, 0)),
    ]
    out_spec = pl.BlockSpec(out_shape.shape, lambda block: (0, 0, 0))
    weight_spec = pl.BlockSpec((chunk_count * 9, CHUNK, slot_count), lambda block: (block, 0, 0))
    grid = (block_count,)
    if kind == "force":
        weight_shape = jax.ShapeDtypeStruct(
            (block_count * chunk_count * 9, CHUNK, slot_count), jnp.float32
        )
        result, weights = pl.pallas_call(
            kernel,
            out_shape=(out_shape, weight_shape),
            grid=grid,
            in_specs=whole,
            out_specs=(out_spec, weight_spec),
        )(target_cols, source_rows)
    elif kind == "jacobi":
        result = pl.pallas_call(kernel, out_shape=out_shape)(target_cols, source_rows, weights)
    else:
        result = pl.pallas_call(
            kernel, out_shape=out_shape, grid=grid, in_specs=whole, out_specs=out_spec
        )(target_cols, source_rows)
    result = result.reshape(output_count, row_count, col_count, slot_count)
    if kind == "force":
        return result, weights
    return result


def shift_lanes(field, distance):
    slot_count = field.shape[-1]
    step = 1
    while step < slot_count:
        rolled = jnp.roll(field, -step, axis=-1)
        chosen = ((distance & step) != 0)[None, :, :, None]
        field = jnp.where(chosen, rolled, field)
        step *= 2
    return field


def place_arrivals(field_six, keep_count, moving):
    slot_count = field_six.shape[3]
    keep_plane = jnp.broadcast_to(keep_count[-1].astype(jnp.float32)[:, None], field_six.shape[2:])
    move_plane = jnp.broadcast_to(moving[-1].astype(jnp.float32)[:, None], field_six.shape[2:])
    edge_pack = jnp.concatenate([field_six[:, -1], keep_plane[None], move_plane[None]], axis=0)
    received = from_behind(edge_pack, "down", 1)
    source_field = jnp.concatenate([received[:6][:, None], field_six[:, :-1]], axis=1)
    source_keep = jnp.concatenate([received[6, :, 0].astype(jnp.int32)[None], keep_count[:-1]], axis=0)
    arriving = jnp.concatenate([received[7, :, 0].astype(jnp.int32)[None], moving[:-1]], axis=0)
    distance = jnp.mod(source_keep - keep_count, slot_count)
    incoming = shift_lanes(source_field, distance)
    incoming = jnp.concatenate([incoming[:1] - 1.0, incoming[1:]], axis=0)
    slot_ids = lax.broadcasted_iota(jnp.int32, field_six.shape[1:], 2)
    own_mask = slot_ids < keep_count[..., None]
    new_mask = (slot_ids >= keep_count[..., None]) & (
        slot_ids < (keep_count + arriving)[..., None]
    )
    return jnp.where(own_mask[None], field_six, jnp.where(new_mask[None], incoming, 0.0))


def per_device(positions, velocities, plastic_viscosity, yield_stress, counts, moving):
    row_count, col_count, slot_count = positions.shape[1:]
    slot_ids = lax.broadcasted_iota(jnp.int32, (row_count, col_count, slot_count), 2)
    live = (slot_ids < counts[:, :, None]).astype(jnp.float32)
    state = jnp.concatenate([positions, velocities, live[None]], axis=0)
    state_pad = with_halo(state, (("down", 1), ("cross", 2)), 1)
    far = jnp.where(state_pad[6:7] > 0.0, state_pad[:3], FAR_AWAY)
    sums = pair_pass(
        "density",
        jnp.concatenate([positions, velocities], axis=0),
        jnp.concatenate([far, state_pad[3:6]], axis=0),
        row_count,
        col_count,
    )
    density = PARTICLE_MASS * (KERNEL_NORM * sums[0] + KERNEL_NORM * (1.0 - live))
    strain = (PARTICLE_MASS * 20.0 * KERNEL_NORM) * sums[1]
    inverse = 1.0 / density
    pressure = STIFFNESS * (density - REST_DENSITY) * inverse * inverse
    viscosity = plastic_viscosity + yield_stress / jnp.sqrt(1.0 + strain)
    dens_pad = with_halo(jnp.stack([inverse, pressure, viscosity]), (("down", 1), ("cross", 2)), 1)
    forces, weights = pair_pass(
        "force",
        jnp.concatenate([positions, pressure[None], viscosity[None]], axis=0),
        jnp.concatenate([far, dens_pad[1:2], dens_pad[0:1], dens_pad[2:3]], axis=0),
        row_count,
        col_count,
    )
    scale = PARTICLE_MASS * 20.0 * KERNEL_NORM
    gravity = jnp.array([GRAVITY_DOWN, 0.0, GRAVITY_UP], jnp.float32)[:, None, None, None]
    predicted = velocities + TIME_STEP * (-scale * forces[:3] + gravity)
    diagonal = 1.0 + TIME_STEP * (scale * inverse * forces[3])
    target = viscosity[None]
    current = predicted
    for sweep_index in range(JACOBI):
        speed_pad = with_halo(current, (("down", 1), ("cross", 2)), 1)
        pulled = pair_pass(
            "jacobi",
            target,
            speed_pad * dens_pad[0:1],
            row_count,
            col_count,
            weights,
        )
        current = (predicted + TIME_STEP * (scale * inverse * pulled)) / diagonal
    moved_positions = positions + TIME_STEP * current
    field_six = jnp.concatenate([moved_positions, current], axis=0)
    keep_count = counts - moving
    result = place_arrivals(field_six, keep_count, moving)
    return (result[:3], result[3:])


def solution(mesh):
    return jax.shard_map(
        per_device,
        mesh=mesh,
        in_specs=(
            P(None, "down", "cross", None),
            P(None, "down", "cross", None),
            P("down", "cross", None),
            P("down", "cross", None),
            P("down", "cross"),
            P("down", "cross"),
        ),
        out_specs=(P(None, "down", "cross", None), P(None, "down", "cross", None)),
        check_vma=False,
    )
```

```python
import math

import jax
import jax.numpy as jnp
from jax import lax
from jax.experimental import pallas as pl
from jax.sharding import PartitionSpec as P

MOVE_MAX = 32
JACOBI = 2


KERNEL_NORM = 21.0 / (2.0 * math.pi)
PARTICLE_MASS = 0.02
REST_DENSITY = 1.0
STIFFNESS = 2.0
TIME_STEP = 0.05
GRAVITY_DOWN = 0.5
GRAVITY_UP = -1.0
NEIGHBOUR_STEPS = [(-1, -1), (-1, 0), (-1, 1), (0, -1), (0, 0), (0, 1), (1, -1), (1, 0), (1, 1)]


def with_halo(array, sides, width):
    for axis, dim in sides:
        count, length = (lax.axis_size(axis), array.shape[dim])
        up = [(i, (i + 1) % count) for i in range(count - 1)]
        down = [(j, i) for i, j in up]
        last = lax.slice_in_dim(array, length - width, length, axis=dim)
        initial = lax.slice_in_dim(array, 0, width, axis=dim)
        before = lax.ppermute(last, axis, up)
        after = lax.ppermute(initial, axis, down)
        array = jnp.concatenate([before, array, after], axis=dim)
    return array


def from_behind(block, axis, distance):
    devices = range(lax.axis_size(axis))
    route = [(i - distance, i) for i in devices if i - distance in devices]
    return lax.ppermute(block, axis, route)


def take_row(padded, lead_blocks, row_index, step_down, step_cross, col_count):
    whole_row = lax.dynamic_index_in_dim(
        padded, row_index + lead_blocks + step_down, axis=1, keepdims=False
    )
    return whole_row[:, lead_blocks + step_cross : lead_blocks + step_cross + col_count, :]


def separation(target, source, step_down, step_cross):
    offsets = (float(step_down), float(step_cross), 0.0)
    separations = [
        source[component][:, None, :] - target[component][:, :, None] + offsets[component]
        for component in range(3)
    ]
    distance = jnp.sqrt(
        separations[0] * separations[0]
        + separations[1] * separations[1]
        + separations[2] * separations[2]
    )
    falloff = jnp.maximum(1.0 - distance, 0.0)
    falloff_cubed = falloff * falloff * falloff
    weight = KERNEL_NORM * falloff_cubed * falloff * (4.0 * distance + 1.0)
    strength = 20.0 * KERNEL_NORM * falloff_cubed
    return (separations, weight, strength)


FAR_AWAY = 1.0e4
CHUNK = 128


def pair_pass(kind, target, source, row_count, col_count, weights=None):
    slot_count = target.shape[-1]
    block_count = row_count * col_count
    chunk_count = slot_count // CHUNK
    padded_cols = col_count + 2
    target_count = target.shape[0]
    source_count = source.shape[0]
    output_count = {"density": 2, "force": 4, "jacobi": 3}[kind]
    target_cols = target.reshape(target_count, block_count, slot_count)
    source_rows = source.reshape(source_count, (row_count + 2) * padded_cols, slot_count)

    def kernel(target_ref, source_ref, *refs):
        if kind == "force":
            out_ref, weight_ref = refs
        elif kind == "jacobi":
            weight_ref, out_ref = refs
        else:
            (out_ref,) = refs

        grid_block = None if kind != "force" else pl.program_id(0)

        def body(step, carry):
            if kind != "force":
                block = step // chunk_count
                first = pl.multiple_of((step % chunk_count) * CHUNK, CHUNK)
            else:
                block = grid_block
                first = pl.multiple_of(step * CHUNK, CHUNK)
            row = block // col_count
            col = block % col_count
            stacked = jnp.zeros((slot_count, slot_count), jnp.float32)
            planes = lax.broadcasted_iota(jnp.int32, (slot_count, slot_count), 0)
            for k in range(target_count):
                stacked = jnp.where(planes == k, target_ref[k, pl.ds(block, 1), :], stacked)
            own = stacked.T
            mine = [
                jnp.broadcast_to(own[:, k : k + 1], (CHUNK, slot_count)) for k in range(target_count)
            ]
            totals = [jnp.zeros((CHUNK, slot_count), jnp.float32) for k in range(output_count)]
            for neighbour, (step_down, step_cross) in enumerate(NEIGHBOUR_STEPS):
                near = (row + 1 + step_down) * padded_cols + (col + 1 + step_cross)
                other = [source_ref[k, pl.ds(near, 1), :] for k in range(source_count)]
                if kind == "jacobi":
                    pull = weight_ref[step * 9 + neighbour]
                    for k in range(3):
                        totals[k] = totals[k] + pull * other[k]
                    continue
                gaps = [
                    other[0] + float(step_down) - mine[0],
                    other[1] + float(step_cross) - mine[1],
                    other[2] - mine[2],
                ]
                squared = gaps[0] * gaps[0] + gaps[1] * gaps[1] + gaps[2] * gaps[2]
                distance = squared * lax.rsqrt(jnp.maximum(squared, 1.0e-30))
                falloff = jnp.maximum(1.0 - distance, 0.0)
                cubed = falloff * falloff * falloff
                if kind == "density":
                    totals[0] = totals[0] + cubed * falloff * (4.0 * distance + 1.0)
                    spread = None
                    for k in range(3):
                        change = other[3 + k] - mine[3 + k]
                        term = change * change
                        spread = term if spread is None else spread + term
                    totals[1] = totals[1] + cubed * spread
                elif kind == "force":
                    push = (mine[3] + other[3]) * cubed
                    for k in range(3):
                        totals[k] = totals[k] + push * gaps[k]
                    pull = (mine[4] + other[5]) * cubed
                    weight_ref[step * 9 + neighbour] = pull
                    totals[3] = totals[3] + pull * other[4]
            lanes = lax.broadcasted_iota(jnp.int32, (CHUNK, slot_count), 1)
            table = jnp.zeros((CHUNK, slot_count), jnp.float32)
            for k in range(output_count):
                table = jnp.where(lanes == k, jnp.sum(totals[k], axis=1, keepdims=True), table)
            flipped = table.T
            for k in range(output_count):
                out_ref[k, pl.ds(block, 1), pl.ds(first, CHUNK)] = flipped[k : k + 1, :]
            return carry

        lax.fori_loop(
            0, block_count * chunk_count if kind != "force" else chunk_count, body, 0, unroll=True
        )

    out_shape = jax.ShapeDtypeStruct((output_count, block_count, slot_count), jnp.float32)
    whole = [
        pl.BlockSpec(target_cols.shape, lambda block: (0, 0, 0)),
        pl.BlockSpec(source_rows.shape, lambda block: (0, 0, 0)),
    ]
    out_spec = pl.BlockSpec(out_shape.shape, lambda block: (0, 0, 0))
    weight_spec = pl.BlockSpec((chunk_count * 9, CHUNK, slot_count), lambda block: (block, 0, 0))
    grid = (block_count,)
    if kind == "force":
        weight_shape = jax.ShapeDtypeStruct(
            (block_count * chunk_count * 9, CHUNK, slot_count), jnp.float32
        )
        result, weights = pl.pallas_call(
            kernel,
            out_shape=(out_shape, weight_shape),
            grid=grid,
            in_specs=whole,
            out_specs=(out_spec, weight_spec),
        )(target_cols, source_rows)
    elif kind == "jacobi":
        result = pl.pallas_call(kernel, out_shape=out_shape)(target_cols, source_rows, weights)
    else:
        result = pl.pallas_call(kernel, out_shape=out_shape)(target_cols, source_rows)
    result = result.reshape(output_count, row_count, col_count, slot_count)
    if kind == "force":
        return result, weights
    return result


def shift_lanes(field, distance):
    slot_count = field.shape[-1]
    step = 1
    while step < slot_count:
        rolled = jnp.roll(field, -step, axis=-1)
        chosen = ((distance & step) != 0)[None, :, :, None]
        field = jnp.where(chosen, rolled, field)
        step *= 2
    return field


def place_arrivals(field_six, keep_count, moving):
    slot_count = field_six.shape[3]
    keep_plane = jnp.broadcast_to(keep_count[-1].astype(jnp.float32)[:, None], field_six.shape[2:])
    move_plane = jnp.broadcast_to(moving[-1].astype(jnp.float32)[:, None], field_six.shape[2:])
    edge_pack = jnp.concatenate([field_six[:, -1], keep_plane[None], move_plane[None]], axis=0)
    received = from_behind(edge_pack, "down", 1)
    source_field = jnp.concatenate([received[:6][:, None], field_six[:, :-1]], axis=1)
    source_keep = jnp.concatenate([received[6, :, 0].astype(jnp.int32)[None], keep_count[:-1]], axis=0)
    arriving = jnp.concatenate([received[7, :, 0].astype(jnp.int32)[None], moving[:-1]], axis=0)
    distance = jnp.mod(source_keep - keep_count, slot_count)
    incoming = shift_lanes(source_field, distance)
    incoming = jnp.concatenate([incoming[:1] - 1.0, incoming[1:]], axis=0)
    slot_ids = lax.broadcasted_iota(jnp.int32, field_six.shape[1:], 2)
    own_mask = slot_ids < keep_count[..., None]
    new_mask = (slot_ids >= keep_count[..., None]) & (
        slot_ids < (keep_count + arriving)[..., None]
    )
    return jnp.where(own_mask[None], field_six, jnp.where(new_mask[None], incoming, 0.0))


def per_device(positions, velocities, plastic_viscosity, yield_stress, counts, moving):
    row_count, col_count, slot_count = positions.shape[1:]
    slot_ids = lax.broadcasted_iota(jnp.int32, (row_count, col_count, slot_count), 2)
    live = (slot_ids < counts[:, :, None]).astype(jnp.float32)
    state = jnp.concatenate([positions, velocities, live[None]], axis=0)
    state_pad = with_halo(state, (("down", 1), ("cross", 2)), 1)
    far = jnp.where(state_pad[6:7] > 0.0, state_pad[:3], FAR_AWAY)
    sums = pair_pass(
        "density",
        jnp.concatenate([positions, velocities], axis=0),
        jnp.concatenate([far, state_pad[3:6]], axis=0),
        row_count,
        col_count,
    )
    density = PARTICLE_MASS * (KERNEL_NORM * sums[0] + KERNEL_NORM * (1.0 - live))
    strain = (PARTICLE_MASS * 20.0 * KERNEL_NORM) * sums[1]
    inverse = 1.0 / density
    pressure = STIFFNESS * (density - REST_DENSITY) * inverse * inverse
    viscosity = plastic_viscosity + yield_stress / jnp.sqrt(1.0 + strain)
    dens_pad = with_halo(jnp.stack([inverse, pressure, viscosity]), (("down", 1), ("cross", 2)), 1)
    forces, weights = pair_pass(
        "force",
        jnp.concatenate([positions, pressure[None], viscosity[None]], axis=0),
        jnp.concatenate([far, dens_pad[1:2], dens_pad[0:1], dens_pad[2:3]], axis=0),
        row_count,
        col_count,
    )
    scale = PARTICLE_MASS * 20.0 * KERNEL_NORM
    gravity = jnp.array([GRAVITY_DOWN, 0.0, GRAVITY_UP], jnp.float32)[:, None, None, None]
    predicted = velocities + TIME_STEP * (-scale * forces[:3] + gravity)
    diagonal = 1.0 + TIME_STEP * (scale * inverse * forces[3])
    target = viscosity[None]
    current = predicted
    for sweep_index in range(JACOBI):
        speed_pad = with_halo(current, (("down", 1), ("cross", 2)), 1)
        pulled = pair_pass(
            "jacobi",
            target,
            speed_pad * dens_pad[0:1],
            row_count,
            col_count,
            weights,
        )
        current = (predicted + TIME_STEP * (scale * inverse * pulled)) / diagonal
    moved_positions = positions + TIME_STEP * current
    field_six = jnp.concatenate([moved_positions, current], axis=0)
    keep_count = counts - moving
    result = place_arrivals(field_six, keep_count, moving)
    return (result[:3], result[3:])


def solution(mesh):
    return jax.shard_map(
        per_device,
        mesh=mesh,
        in_specs=(
            P(None, "down", "cross", None),
            P(None, "down", "cross", None),
            P("down", "cross", None),
            P("down", "cross", None),
            P("down", "cross"),
            P("down", "cross"),
        ),
        out_specs=(P(None, "down", "cross", None), P(None, "down", "cross", None)),
        check_vma=False,
    )
```
